128 devices in a mesh: blk: 8 (over z, core), grp: 16 (over x, y).
Axes of the slice: x: 4, y: 4, z: 4, core: 2. Of those that a mesh axis runs over, the one named last changes fastest.
Arguments:
- user_prior: float32 [32768, 128], P(('blk', 'grp')), may hold values from -6 to 6
- item_factors: bfloat16 [524288, 128], P(('blk', 'grp')), may hold values from -0.375 to 0.375
- user_tiles: int32 [8192], P(('blk', 'grp')), may hold values from 0 to 31
- item_tiles: int32 [8192], P(('blk', 'grp')), may hold values from 0 to 4095, as said below
- counts: int32 [8192, 128, 128], P(('blk', 'grp')), may hold values from 0 to 20, as said below
Outputs:
- user_factors: float32 [32768, 128], P(('blk', 'grp'))
The draws below stay inside these ranges and needn't reach their ends.
Inputs may be any that keep to these rules, and one draw needn't show every extreme that they name: `item_tiles`: item tile t is held by device t // 32 of blk+grp. The entries of one device name tiles of 32 different holders, exactly 2 entries for each holder that they name, in no particular order. In each device's 64 entries, those whose tile of counts has a nonzero value come before those whose tile is all zero; in every group along grp at least one device has all 64 entries of the first kind.
All inputs are finite; a program needn't handle non-finite values.
Results may differ from the reference program's by a relative error of at most 0.0003.
The reference program's roundings to bfloat16 on the way count: a program that leaves them out, or rounds other values in their place, can miss the bound.
Values may be sent and summed in bfloat16 or wider, within the bound.
A program may use at most 128 MiB of HBM per device.

```python
import jax
import jax.numpy as jnp
from jax import lax

R = 128
TILE = 128
ITERS = 3
UTB = 32
PAIRS_DEV = 64
IT_DEV = 32
CAP = 2
PAIRS = 8192
ITEM_TILES = 4096
ITEMS = 524288
USERS = 32768
N_BLK = 8
N_GRP = 16


def draw_item_tiles(key, part):
    devices = N_BLK * N_GRP
    holders = PAIRS_DEV // CAP
    device_keys = jax.random.split(jax.random.fold_in(key, 11), devices)

    def one_device(device_key):
        order_key, slot_key, place_key = jax.random.split(device_key, 3)
        owners = jax.random.permutation(order_key, devices)[:holders]
        owner_of = jnp.repeat(owners, CAP, total_repeat_length=PAIRS_DEV)
        owner_of = owner_of[jax.random.permutation(place_key, PAIRS_DEV)]
        slots = jax.random.randint(slot_key, (PAIRS_DEV,), 0, IT_DEV)
        return (owner_of * IT_DEV + slots).astype(jnp.int32)
    return jax.vmap(one_device)(device_keys).reshape(-1)


def draw_counts(key, part):
    devices = N_BLK * N_GRP
    shift_key, full_key, value_key, first_key = jax.random.split(jax.random.fold_in(key, 23), 4)
    shifts = jax.random.randint(shift_key, (devices,), 0, 4)
    full_slot = jax.random.randint(full_key, (N_BLK,), 0, N_GRP)
    device_ids = jnp.arange(devices, dtype=jnp.int32)
    is_full = device_ids % N_GRP == full_slot[device_ids // N_GRP]
    live = jnp.where(is_full, PAIRS_DEV, jnp.right_shift(jnp.full((devices,), PAIRS_DEV, jnp.int32), shifts))
    position = jnp.arange(PAIRS_DEV, dtype=jnp.int32)
    live_mask = (position[None, :] < live[:, None]).astype(jnp.int32).reshape(-1)
    raw = jax.random.randint(value_key, (devices * PAIRS_DEV, TILE, TILE), 0, 4000)
    values = jnp.where(raw < 3980, 0, raw - 3979)
    first = jax.random.randint(first_key, (devices * PAIRS_DEV,), 1, 21)
    values = values.at[:, 0, 0].set(first)
    return (values * live_mask[:, None, None]).astype(jnp.int32)


def set_ends(values, rng, least, largest):
    extent = values.shape
    spot = [jax.random.randint(jax.random.fold_in(rng, axis), (), 0, extent[axis]) for axis in range(len(extent))]
    values = values.at[tuple(spot)].set(least)
    longest = extent.index(max(extent))
    spot[longest] = (spot[longest] + 1) % extent[longest]
    return values.at[tuple(spot)].set(largest)


def raised(values, rng, source, target, shards_of, factor):
    owner, partner = [(jnp.arange(values.shape[dim]) // (values.shape[dim] // shards_of)).reshape([-1 if axis == dim else 1 for axis in range(values.ndim)]) for dim in (source, target)]
    chosen = jax.random.permutation(rng, shards_of)[partner]
    strong = (owner == chosen) | (owner == (partner + shards_of // 2) % shards_of)
    return jnp.where(strong, factor * values, values)


def level_of(key, shape, cuts, least, largest):
    def one(dim, blocks):
        heights = jax.random.uniform(jax.random.fold_in(jax.random.fold_in(key, 6), dim), (blocks,), jnp.float32, least / len(cuts), largest / len(cuts))
        return jnp.repeat(jnp.exp(heights), shape[dim] // blocks).reshape((-1,) + (1,) * (len(shape) - dim - 1))

    factor_of = one(*cuts[0])
    for cut in cuts[1:]:
        factor_of = factor_of * one(*cut)
    return factor_of


def centred(own_key, shape, spread, reach, cuts=(), held_as=jnp.bfloat16):
    loudness = level_of(own_key, shape, cuts, -0.22, 0.18) if cuts else 1.0
    result = jax.random.normal(own_key, shape, jnp.float32) * spread * loudness
    return jnp.minimum(jnp.maximum(result, -reach), reach).astype(held_as)


def noise_with(key, extent, spread, reach, shards, heavy, kind=jnp.bfloat16):
    array = spread * jax.random.normal(key, extent, jnp.float32)
    if shards:
        array = array * level_of(key, extent, shards, -0.22, 0.18)
    return jnp.clip(raised(array, jax.random.fold_in(key, 3), *heavy), -reach, reach).astype(kind)


def setup_inputs(seed: int = 0) -> dict:
    seeds = jax.random.split(jax.random.key(seed), 6)
    user_prior = centred(seeds[0], (USERS, R), 1.0, 6.0, ((0, 128),), jnp.float32)
    item_factors = noise_with(seeds[1], (ITEMS, R), (32 * R) ** -0.5, 0.375, ((0, 128),), (0, 1, 128, 5.5))
    user_tiles = set_ends(jax.random.randint(seeds[2], (PAIRS,), 0, UTB), jax.random.fold_in(seeds[2], 1), 0, UTB - 1).astype(jnp.int32)
    item_tiles = draw_item_tiles(jax.random.fold_in(seeds[5], 71), 0)
    counts = draw_counts(jax.random.fold_in(seeds[5], 71), 0)
    return dict(user_prior=user_prior, item_factors=item_factors, user_tiles=user_tiles, item_tiles=item_tiles, counts=counts)


ALPHA = 40.0
REG = 32.0
EPS = 1e-6


def pair_products(low_tiles, factor_tiles, user_ids, item_ids, count_sets, with_rhs):
    def step(totals, inputs):
        users, items, counted = inputs
        factors = factor_tiles[items].astype(jnp.float32)
        counted = counted.astype(jnp.float32)
        if with_rhs:
            weights = jnp.where(counted > 0, 1.0 + ALPHA * counted, 0.0).astype(jnp.bfloat16)
        else:
            users_low = low_tiles[users].astype(jnp.float32)
            scores = jnp.einsum("bur,bir->bui", users_low, factors)
            weights = (ALPHA * counted * scores).astype(jnp.bfloat16)
        weights = lax.optimization_barrier(weights).astype(jnp.float32)
        back = jnp.einsum("bui,bir->bur", weights, factors)
        return totals.at[users].add(back), None

    start = jnp.zeros((UTB * N_BLK, TILE, R), jnp.float32)
    totals, _ = lax.scan(step, start, (user_ids, item_ids, count_sets))
    return totals.reshape(USERS, R)


def reference(user_prior, item_factors, user_tiles, item_tiles, counts):
    devices = N_BLK * N_GRP
    gram = lax.dot_general(item_factors, item_factors, (((0,), (0,)), ((), ())), preferred_element_type=jnp.float32)
    factor_tiles = item_factors.reshape(ITEM_TILES, TILE, R)
    offsets = (jnp.arange(devices, dtype=jnp.int32) // N_GRP) * UTB
    user_ids = user_tiles.reshape(devices, PAIRS_DEV) + offsets[:, None]
    item_ids = item_tiles.reshape(devices, PAIRS_DEV)
    count_sets = counts.reshape(devices, PAIRS_DEV, TILE, TILE)

    def operate(vectors):
        low_tiles = vectors.astype(jnp.bfloat16).reshape(UTB * N_BLK, TILE, R)
        pairs = pair_products(low_tiles, factor_tiles, user_ids, item_ids, count_sets, False)
        return jnp.dot(vectors, gram, precision=lax.Precision.HIGHEST) + REG * vectors + pairs

    rhs = pair_products(None, factor_tiles, user_ids, item_ids, count_sets, True)
    solution = user_prior
    residual = rhs - operate(solution)
    direction = residual
    norm_now = jnp.sum(residual * residual, axis=1, keepdims=True)
    for step in range(ITERS):
        image = operate(direction)
        alpha = norm_now / (jnp.sum(direction * image, axis=1, keepdims=True) + EPS)
        solution = solution + alpha * direction
        residual = residual - alpha * image
        fresh = jnp.sum(residual * residual, axis=1, keepdims=True)
        direction = residual + (fresh / (norm_now + EPS)) * direction
        norm_now = fresh
    return solution
```

```python
import functools

import jax
import jax.numpy as jnp
from jax import lax
from jax.experimental import pallas as pl
from jax.experimental.pallas import tpu as pltpu
from jax.sharding import PartitionSpec as P

ITERS = 3
ALPHA = 40.0
REG = 32.0
EPS = 1e-06
SIDE = 4
MESH = pl.DeviceIdType.MESH
STRIDE = 53


def coords():
    b = lax.axis_index("blk")
    g = lax.axis_index("grp")
    return b, g, g // SIDE, g % SIDE


def row_col(axis, k):
    b, g, x, y = coords()
    if axis == 0:
        return b, ((x + k) % SIDE) * SIDE + y
    return b, x * SIDE + (y + k) % SIDE


def remote(src, dst, send_sem, recv_sem, device):
    return pltpu.make_async_remote_copy(
        src_ref=src, dst_ref=dst, send_sem=send_sem, recv_sem=recv_sem,
        device_id=device, device_id_type=MESH,
    )


def tile_place(u):
    g = u // 2
    x, y = g // SIDE, g % SIDE
    return jnp.where(u % 2 == 0, y * SIDE + x, SIDE * SIDE + x * SIDE + y)


def gather_first(low, sems):
    _, _, x, y = coords()
    copies = []
    for k in range(1, SIDE):
        for t in range(2):
            place = y * SIDE + x if t == 0 else SIDE * SIDE + x * SIDE + y
            copies.append(remote(
                low.at[place], low.at[place], sems.at[0, 0, t, k], sems.at[0, 1, t, k],
                row_col(t, k),
            ))
    return copies


def gather_second(low, sems):
    _, _, x, y = coords()
    copies = []
    for k in range(1, SIDE):
        for t in range(2):
            start = y * SIDE if t == 0 else SIDE * SIDE + x * SIDE
            copies.append(remote(
                low.at[pl.ds(start, SIDE)], low.at[pl.ds(start, SIDE)],
                sems.at[1, 0, t, k], sems.at[1, 1, t, k], row_col(1 - t, k),
            ))
    return copies


def fetch_kernel(
    n_blk, n_grp,
    wanted_tiles, user_tiles, items, prior, counts,
    out_tiles, out_gram, out_low, out_weights, out_index,
    req, reqs, want, want_s, sel, sel_s, send, recv, low, gram_own, gram_a, gram_b, gram_c, gram_t,
    req_sems, tile_sems, low_sems, gram_sems, local_sem,
):
    n_all = n_blk * n_grp
    b, g, x, y = coords()
    me = b * n_grp + g
    pairs = out_tiles.shape[0]
    held = items.shape[0]
    tile = items.shape[1]
    rank = items.shape[2]

    def peer(step):
        shift = (step * STRIDE) % n_all
        db, dg = shift % n_blk, shift // n_blk
        dc, dz = db % 2, db // 2
        dx, dy = dg // SIDE, dg % SIDE
        nb = ((b // 2 + dz) % (n_blk // 2)) * 2 + (b % 2 + dc) % 2
        ng = ((x + dx) % SIDE) * SIDE + (y + dy) % SIDE
        return nb, ng

    barrier = pltpu.get_barrier_semaphore()

    def greet(step, carry):
        pl.semaphore_signal(barrier, inc=1, device_id=peer(step), device_id_type=MESH)
        return carry

    lax.fori_loop(1, n_all, greet, 0)

    lane = lax.broadcasted_iota(jnp.int32, (1, 128), 1)

    def ask(p, state):
        first, second, seen, order, last, before = state
        entry = wanted_tiles[p]
        owner, slot = entry // held, entry % held
        hit = lane == owner
        fresh = jnp.logical_and(hit, seen == 0)
        turn = jnp.sum(jnp.where(hit, seen, 0), axis=1, keepdims=True)
        order = jnp.where(lane == p, owner * 2 + jnp.minimum(turn, 1), order)
        first = jnp.where(fresh, slot, first)
        second = jnp.where(hit, slot, second)
        seen = jnp.where(hit, 1, seen)
        mine = lane == user_tiles[p]
        earlier = jnp.sum(jnp.where(mine, last, 0), axis=1, keepdims=True)
        before = jnp.where(lane == p, earlier, before)
        last = jnp.where(mine, p + 1, last)
        return first, second, seen, order, last, before

    zero = jnp.zeros((1, 128), jnp.int32)
    first, second, _, order, last, before = lax.fori_loop(0, pairs, ask, (zero,) * 6)
    row = lax.broadcasted_iota(jnp.int32, (8, 128), 0)
    req[...] = jnp.where(row == 0, first, jnp.where(row == 1, second, 0))
    sel[...] = jnp.where(row == 0, order, 0)
    out_index[...] = jnp.where(row == 0, before, jnp.where(row == 1, last, 0))
    reqs[me] = req[...]
    pltpu.make_async_copy(sel, sel_s, local_sem).start()
    low[y * SIDE + x] = prior[0].astype(jnp.bfloat16)
    low[SIDE * SIDE + x * SIDE + y] = prior[1].astype(jnp.bfloat16)
    pltpu.make_async_copy(sel, sel_s, local_sem).wait()

    pl.semaphore_wait(barrier, n_all - 1)

    def request(step):
        nb, ng = peer(step)
        return remote(req, reqs.at[me], req_sems.at[0, step], req_sems.at[1, step], (nb, ng))

    def send_request(step, carry):
        request(step).start()
        return carry

    lax.fori_loop(1, n_all, send_request, 0)

    gathers = gather_first(low, low_sems)
    for copy in gathers:
        copy.start()

    chunk = min(8, held)

    def gram_step(i, total):
        block = items[pl.ds(i * chunk, chunk)].reshape(chunk * tile, rank)
        return total + lax.dot_general(
            block, block, (((0,), (0,)), ((), ())), preferred_element_type=jnp.float32
        )

    gram_rows = rank // n_grp
    gram_own[...] = lax.fori_loop(
        0, held // chunk, gram_step, jnp.zeros((rank, rank), jnp.float32)
    ).reshape(n_grp, gram_rows, rank)

    def gram_first(k):
        ng = (g + k) % n_grp
        return remote(
            gram_own.at[ng], gram_a.at[k], gram_sems.at[0, 0, k], gram_sems.at[0, 1, k], (b, ng)
        )

    for k in range(1, n_grp):
        gram_first(k).start()

    def wait_request(step, carry):
        request(step).wait_send()
        request(step).wait_recv()
        return carry

    lax.fori_loop(1, n_all, wait_request, 0)

    def collect(d, total):
        mine = jnp.sum(jnp.where(lane == me, reqs[d], 0), axis=1, keepdims=True)
        return jnp.where(lane == d, mine, total)

    want[...] = lax.fori_loop(0, n_all, collect, jnp.zeros((8, 128), jnp.int32))
    pltpu.make_async_copy(want, want_s, local_sem).start()

    for k in range(1, n_grp):
        gram_first(k).wait()
    part = gram_own[g]
    for k in range(1, n_grp):
        part = part + gram_a[k]
    gram_t[0] = part
    pltpu.make_async_copy(want, want_s, local_sem).wait()

    def gram_second(k):
        return remote(
            gram_t.at[0], gram_b.at[k], gram_sems.at[1, 0, k], gram_sems.at[1, 1, k],
            ((b + k) % n_blk, g),
        )

    for k in range(1, n_blk):
        gram_second(k).start()

    for copy in gathers:
        copy.wait()
    gathers = gather_second(low, low_sems)
    for copy in gathers:
        copy.start()

    def pack(step):
        nb, ng = peer(step)
        to = nb * n_grp + ng
        send[step, 0] = items[want_s[0, to]]
        send[step, 1] = items[want_s[1, to]]

    def parcel(step):
        return remote(
            send.at[step], recv.at[me], tile_sems.at[0, step], tile_sems.at[1, step], peer(step)
        )

    def ship(step, carry):
        @pl.when(step + 1 < n_all)
        def _():
            pack(step + 1)

        parcel(step).start()
        return carry

    pack(1)
    half = n_all // 4
    lax.fori_loop(1, half, ship, 0)

    for k in range(1, n_blk):
        gram_second(k).wait()
    part = gram_t[0]
    for k in range(1, n_blk):
        part = part + gram_b[k]
    gram_t[1] = part
    gram_c[g] = part

    def gram_third(k):
        return remote(
            gram_t.at[1], gram_c.at[g], gram_sems.at[2, 0, k], gram_sems.at[2, 1, k],
            (b, (g + k) % n_grp),
        )

    lax.fori_loop(half, n_all, ship, 0)
    for k in range(1, n_grp):
        gram_third(k).start()
    recv[me, 0] = items[want_s[0, me]]
    recv[me, 1] = items[want_s[1, me]]

    def weigh(p, carry):
        out_weights[p] = (counts[p].astype(jnp.float32) * ALPHA).astype(jnp.bfloat16)
        return carry

    lax.fori_loop(0, pairs, weigh, 0)

    for copy in gathers:
        copy.wait()
    out_low[...] = low[...]
    for k in range(1, n_grp):
        gram_third(k).wait()
    out_gram[...] = gram_c[...].reshape(rank, rank)

    def wait_parcel(step, carry):
        parcel(step).wait_send()
        parcel(step).wait_recv()
        return carry

    lax.fori_loop(1, n_all, wait_parcel, 0)

    def take(p, carry):
        place = sel_s[0, p]
        out_tiles[p] = recv[place // 2, place % 2]
        return carry

    lax.fori_loop(0, pairs, take, 0)


def sweep_kernel(
    user_tiles, index, tiles, gram, low_in, weights, prior,
    out,
    chain, low, parts, first_in, sums, second_in, residual, direction,
    low_sems, sum_sems,
):
    pairs, tile, rank = tiles.shape
    _, _, x, y = coords()
    users = SIDE * SIDE * 2

    barrier = pltpu.get_barrier_semaphore()
    for k in range(1, SIDE):
        for axis in range(2):
            pl.semaphore_signal(barrier, inc=1, device_id=row_col(axis, k), device_id_type=MESH)

    chain[0] = jnp.zeros((tile, rank), jnp.float32)
    low[...] = low_in[...]

    def accumulate(with_rhs):
        group = 4

        def several(i, carry):
            backs = []
            for j in range(group):
                p = i * group + j
                factors = tiles[p]
                weight = weights[p].astype(jnp.float32)
                scores = lax.dot_general(
                    low[tile_place(user_tiles[p])], factors, (((1,), (1,)), ((), ())),
                    preferred_element_type=jnp.float32,
                )
                scaled = (weight * scores).astype(jnp.bfloat16)
                back = jnp.dot(scaled, factors, preferred_element_type=jnp.float32)
                if with_rhs:
                    confidence = jnp.where(weight > 0, 1.0 + weight, 0.0).astype(jnp.bfloat16)
                    back = jnp.dot(
                        confidence, factors, preferred_element_type=jnp.float32
                    ) - back
                backs.append(back)
            for j in range(group):
                p = i * group + j
                chain[p + 1] = chain[index[0, p]] + backs[j]
            return carry

        lax.fori_loop(0, pairs // group, several, 0)

        def final(u, carry):
            parts[tile_place(u)] = chain[index[1, u]]
            return carry

        lax.fori_loop(0, users, final, 0)

    def sum_first(k, t):
        away = (y + k) % SIDE if t == 0 else (x + k) % SIDE
        return remote(
            parts.at[pl.ds(t * SIDE * SIDE + away * SIDE, SIDE)], first_in.at[t, k],
            sum_sems.at[0, 0, t, k], sum_sems.at[0, 1, t, k], row_col(1 - t, k),
        )

    def sum_second(k, t):
        away = (x + k) % SIDE if t == 0 else (y + k) % SIDE
        return remote(
            sums.at[t, away], second_in.at[t, k],
            sum_sems.at[1, 0, t, k], sum_sems.at[1, 1, t, k], row_col(t, k),
        )

    def reduce_start():
        for k in range(1, SIDE):
            for t in range(2):
                sum_first(k, t).start()

    def reduce_finish():
        for k in range(1, SIDE):
            for t in range(2):
                sum_first(k, t).wait()
        for t in range(2):
            near = y if t == 0 else x
            for j in range(SIDE):
                total = parts[t * SIDE * SIDE + near * SIDE + j]
                for k in range(1, SIDE):
                    total = total + first_in[t, k, j]
                sums[t, j] = total
        for k in range(1, SIDE):
            for t in range(2):
                sum_second(k, t).start()
        for k in range(1, SIDE):
            for t in range(2):
                sum_second(k, t).wait()
        totals = []
        for t in range(2):
            total = sums[t, x if t == 0 else y]
            for k in range(1, SIDE):
                total = total + second_in[t, k]
            totals.append(total)
        return jnp.concatenate(totals, axis=0)

    def gram_term(vectors):
        return (
            jnp.dot(vectors, gram[...], precision=lax.Precision.HIGHEST,
                    preferred_element_type=jnp.float32)
            + REG * vectors
        )

    def row_sum(left, right):
        return jnp.sum(left * right, axis=1, keepdims=True)

    accumulate(True)
    pl.semaphore_wait(barrier, 2 * (SIDE - 1))
    reduce_start()
    local = gram_term(prior[...])
    start = reduce_finish() - local
    residual[...] = start
    direction[...] = start
    out[...] = prior[...]

    def iterate(step, norm_now):
        d = direction[...]
        d_low = d.astype(jnp.bfloat16)
        low[y * SIDE + x] = d_low[:tile]
        low[SIDE * SIDE + x * SIDE + y] = d_low[tile:]
        copies = gather_first(low, low_sems)
        for copy in copies:
            copy.start()
        for copy in copies:
            copy.wait()
        copies = gather_second(low, low_sems)
        for copy in copies:
            copy.start()
        for copy in copies:
            copy.wait()
        accumulate(False)
        reduce_start()
        local = gram_term(direction[...])
        image = local + reduce_finish()
        d = direction[...]
        alpha = norm_now / (row_sum(d, image) + EPS)
        out[...] = out[...] + alpha * d
        r = residual[...] - alpha * image
        residual[...] = r
        fresh = row_sum(r, r)
        direction[...] = r + fresh / (norm_now + EPS) * d
        return fresh

    lax.fori_loop(0, ITERS, iterate, row_sum(start, start))


def body(user_prior, item_factors, user_tiles, item_tiles, counts):
    n_blk = lax.axis_size("blk")
    n_grp = lax.axis_size("grp")
    n_all = n_blk * n_grp
    pairs, tile, _ = counts.shape
    rank = item_factors.shape[1]
    users = 2 * n_grp
    own = user_prior.shape[0]
    held = item_factors.shape[0] // tile
    vmem = pl.BlockSpec(memory_space=pltpu.VMEM)
    smem = pl.BlockSpec(memory_space=pltpu.SMEM)
    dma = pltpu.SemaphoreType.DMA
    items = item_factors.reshape(held, tile, rank)
    prior = user_prior.reshape(2, tile, rank)
    tiles, gram, low, weights, index = pl.pallas_call(
        functools.partial(fetch_kernel, n_blk, n_grp),
        out_shape=(
            jax.ShapeDtypeStruct((pairs, tile, rank), jnp.bfloat16),
            jax.ShapeDtypeStruct((rank, rank), jnp.float32),
            jax.ShapeDtypeStruct((users, tile, rank), jnp.bfloat16),
            jax.ShapeDtypeStruct((pairs, tile, tile), jnp.bfloat16),
            jax.ShapeDtypeStruct((8, 128), jnp.int32),
        ),
        in_specs=[smem, smem, vmem, vmem, vmem],
        out_specs=(vmem,) * 5,
        scratch_shapes=[
            pltpu.VMEM((8, 128), jnp.int32),
            pltpu.VMEM((n_all, 8, 128), jnp.int32),
            pltpu.VMEM((8, 128), jnp.int32),
            pltpu.SMEM((8, 128), jnp.int32),
            pltpu.VMEM((8, 128), jnp.int32),
            pltpu.SMEM((8, 128), jnp.int32),
            pltpu.VMEM((n_all, 2, tile, rank), jnp.bfloat16),
            pltpu.VMEM((n_all, 2, tile, rank), jnp.bfloat16),
            pltpu.VMEM((users, tile, rank), jnp.bfloat16),
            pltpu.VMEM((n_grp, rank // n_grp, rank), jnp.float32),
            pltpu.VMEM((n_grp, rank // n_grp, rank), jnp.float32),
            pltpu.VMEM((n_blk, rank // n_grp, rank), jnp.float32),
            pltpu.VMEM((n_grp, rank // n_grp, rank), jnp.float32),
            pltpu.VMEM((2, rank // n_grp, rank), jnp.float32),
            dma((2, n_all)),
            dma((2, n_all)),
            dma((2, 2, 2, SIDE)),
            dma((3, 2, n_grp)),
            dma,
        ],
        compiler_params=pltpu.CompilerParams(
            collective_id=0, has_side_effects=True, vmem_limit_bytes=60 << 20
        ),
        name="fetch",
    )(item_tiles, user_tiles, items, prior, counts)

    return pl.pallas_call(
        sweep_kernel,
        out_shape=jax.ShapeDtypeStruct((own, rank), jnp.float32),
        in_specs=[smem, smem, vmem, vmem, vmem, vmem, vmem],
        out_specs=vmem,
        scratch_shapes=[
            pltpu.VMEM((pairs + 1, tile, rank), jnp.float32),
            pltpu.VMEM((users, tile, rank), jnp.bfloat16),
            pltpu.VMEM((users, tile, rank), jnp.float32),
            pltpu.VMEM((2, SIDE, SIDE, tile, rank), jnp.float32),
            pltpu.VMEM((2, SIDE, tile, rank), jnp.float32),
            pltpu.VMEM((2, SIDE, tile, rank), jnp.float32),
            pltpu.VMEM((own, rank), jnp.float32),
            pltpu.VMEM((own, rank), jnp.float32),
            dma((2, 2, 2, SIDE)),
            dma((2, 2, 2, SIDE)),
        ],
        compiler_params=pltpu.CompilerParams(
            collective_id=1, has_side_effects=True, vmem_limit_bytes=60 << 20
        ),
        name="sweep",
    )(user_tiles, index, tiles, gram, low, weights, user_prior)


def solution(mesh):
    in_specs = (
        P(("blk", "grp"), None),
        P(("blk", "grp"), None),
        P(("blk", "grp")),
        P(("blk", "grp")),
        P(("blk", "grp"), None, None),
    )
    out_specs = P(("blk", "grp"), None)
    return jax.shard_map(body, mesh=mesh, in_specs=in_specs, out_specs=out_specs, check_vma=False)
```

```python
import functools

import jax
import jax.numpy as jnp
from jax import lax
from jax.experimental import pallas as pl
from jax.experimental.pallas import tpu as pltpu
from jax.sharding import PartitionSpec as P

ITERS = 3
ALPHA = 40.0
REG = 32.0
EPS = 1e-06
SIDE = 4
PLANE = SIDE * SIDE
FACE = 2 * PLANE
LEVELS = 32700.0
SHARE = ((0, 48), (48, 48), (96, 32))
MESH = pl.DeviceIdType.MESH


def position():
    b = lax.axis_index("blk")
    g = lax.axis_index("grp")
    return (g // SIDE, g % SIDE, b // 2), b % 2


def mesh_id(place, core):
    x, y, z = place
    return z * 2 + core, x * SIDE + y


def flat_id(place, core):
    b, g = mesh_id(place, core)
    return b * PLANE + g


def moved(place, axis, k):
    return tuple((v + k) % SIDE if i == axis else v for i, v in enumerate(place))


def put_at(place, axis, value):
    return tuple(value if i == axis else v for i, v in enumerate(place))


def remote(src, dst, send_sem, recv_sem, device):
    return pltpu.make_async_remote_copy(
        src_ref=src, dst_ref=dst, send_sem=send_sem, recv_sem=recv_sem,
        device_id=device, device_id_type=MESH,
    )


def quantize(value):
    top = jnp.maximum(jnp.max(jnp.abs(value), axis=0, keepdims=True), 1e-30)
    whole = jnp.round(value * (LEVELS / top)).astype(jnp.int32).astype(jnp.int16)
    return whole, top * (1.0 / LEVELS)


def restore(whole, unit):
    return whole.astype(jnp.int32).astype(jnp.float32) * unit


def tile_place(u):
    g = u // 2
    x, y = g // SIDE, g % SIDE
    return jnp.where(u % 2 == 0, y * SIDE + x, PLANE + x * SIDE + y)


def kernel(
    n_blk, n_grp,
    wanted_tiles, user_tiles, items, prior, counts,
    out,
    req, reqs, want, table, table_s,
    ring0, ring1, ring2, send0, send1, send2, recv0, recv1, recv2,
    tiles, counted, weights, low, chain,
    gram_own, gram_a, gram_b, gram_c, gram_t,
    part_q, part_u, first_q, first_u, sum_q, sum_u, second_q, second_u, sums,
    residual, direction, local,
    req_sems, ring_sems, tile_sems, gather_one, gather_two, first_sems, second_sems,
    gram_sems, local_sems,
):
    n_all = n_blk * n_grp
    place, core = position()
    x, y, z = place
    b, g = mesh_id(place, core)
    me = b * n_grp + g
    pairs, tile, rank = tiles.shape
    held = items.shape[0]
    rings, sends, recvs = (ring0, ring1, ring2), (send0, send1, send2), (recv0, recv1, recv2)

    count_copy = pltpu.make_async_copy(counts, counted, local_sems.at[0])
    count_copy.start()

    def other(step):
        b_to = (b + step // n_grp) % n_blk
        return b_to, (g + step % n_grp) % n_grp

    barrier = pltpu.get_barrier_semaphore()

    def greet(step, carry):
        pl.semaphore_signal(barrier, inc=1, device_id=other(step), device_id_type=MESH)
        return carry

    lax.fori_loop(1, n_all, greet, 0)

    lane = lax.broadcasted_iota(jnp.int32, (1, 128), 1)
    zero = jnp.zeros((1, 128), jnp.int32)

    def ask(i, state):
        first, second = state
        for j in range(8):
            p = i * 8 + j
            late, early = wanted_tiles[p], wanted_tiles[pairs - 1 - p]
            second = jnp.where(lane == late // held, late % held, second)
            first = jnp.where(lane == early // held, early % held, first)
        return first, second

    first, second = lax.fori_loop(0, pairs // 8, ask, (zero, zero))
    asked = first + 256 * second
    req[...] = asked
    reqs[me] = asked
    low[y * SIDE + x] = prior[:tile].astype(jnp.bfloat16)
    low[PLANE + x * SIDE + y] = prior[tile:].astype(jnp.bfloat16)

    def keep(i, carry):
        for axis, (start, rows) in enumerate(SHARE):
            rings[axis][place[axis], i] = items[i, start:start + rows]
        return carry

    lax.fori_loop(0, held, keep, 0)

    pl.semaphore_wait(barrier, n_all - 1)

    def request(step):
        return remote(
            req, reqs.at[me], req_sems.at[0, step], req_sems.at[1, step], other(step)
        )

    def send_request(step, carry):
        request(step).start()
        return carry

    lax.fori_loop(1, n_all, send_request, 0)

    def ring_copy(axis, kind):
        start, rows = SHARE[axis]
        ring = rings[axis]
        here = place[axis]
        if kind < 2:
            src, dst = items.at[:, pl.ds(start, rows)], ring.at[here]
        else:
            origin = (here + SIDE - 1) % SIDE if kind == 2 else (here + 1) % SIDE
            half = pl.ds(0 if kind == 2 else held // 2, held // 2)
            src = dst = ring.at[origin, half]
        to = moved(place, axis, 1 if kind % 2 == 0 else SIDE - 1)
        return remote(
            src, dst, ring_sems.at[0, axis, kind], ring_sems.at[1, axis, kind],
            mesh_id(to, core),
        )

    for kind in range(2):
        for axis in range(3):
            ring_copy(axis, kind).start()

    def low_place(t, m):
        if t == 0:
            return y * SIDE + (x + SIDE - m) % SIDE
        return PLANE + x * SIDE + (y + SIDE - m) % SIDE

    def gather_a(t, k):
        ref = low.at[low_place(t, 0)]
        return remote(
            ref, ref, gather_one.at[0, t, k], gather_one.at[1, t, k],
            mesh_id(moved(place, t, k), core),
        )

    def gather_b(t, k, m):
        ref = low.at[low_place(t, m)]
        return remote(
            ref, ref, gather_two.at[0, t, k, m], gather_two.at[1, t, k, m],
            mesh_id(moved(place, 1 - t, k), core),
        )

    def gather_begin():
        for k in range(1, SIDE):
            for t in range(2):
                gather_a(t, k).start()
        for k in range(1, SIDE):
            for t in range(2):
                gather_b(t, k, 0).start()

    def gather_onward():
        for m in range(1, SIDE):
            for t in range(2):
                gather_a(t, m).wait()
                for k in range(1, SIDE):
                    gather_b(t, k, m).start()

    def gather_end():
        for m in range(SIDE):
            for k in range(1, SIDE):
                for t in range(2):
                    gather_b(t, k, m).wait()

    gather_begin()

    chunk = min(8, held)

    def gram_step(i, total):
        block = items[pl.ds(i * chunk, chunk)].reshape(chunk * tile, rank)
        return total + lax.dot_general(
            block, block, (((0,), (0,)), ((), ())), preferred_element_type=jnp.float32
        )

    gram_own[...] = lax.fori_loop(
        0, held // chunk, gram_step, jnp.zeros((rank, rank), jnp.float32)
    ).reshape(n_grp, rank // n_grp, rank)

    def gram_first(k):
        to = (g + k) % n_grp
        return remote(
            gram_own.at[to], gram_a.at[k], gram_sems.at[0, 0, k], gram_sems.at[0, 1, k], (b, to)
        )

    def gram_second(k):
        return remote(
            gram_t.at[0], gram_b.at[k], gram_sems.at[1, 0, k], gram_sems.at[1, 1, k],
            ((b + k) % n_blk, g),
        )

    def gram_third(k):
        return remote(
            gram_t.at[1], gram_c.at[g], gram_sems.at[2, 0, k], gram_sems.at[2, 1, k],
            (b, (g + k) % n_grp),
        )

    for k in range(1, n_grp):
        gram_first(k).start()

    for axis in range(3):
        for kind in range(2):
            ring_copy(axis, kind).wait()
            ring_copy(axis, kind + 2).start()

    gather_onward()

    def wait_request(step, carry):
        request(step).wait()
        return carry

    lax.fori_loop(1, n_all, wait_request, 0)
    want_copy = pltpu.make_async_copy(reqs, want, local_sems.at[1])
    want_copy.start()
    for k in range(1, n_grp):
        gram_first(k).wait()
    part = gram_own[g]
    for k in range(1, n_grp):
        part = part + gram_a[k]
    gram_t[0] = part
    want_copy.wait()
    for k in range(1, n_blk):
        gram_second(k).start()
    for axis in range(3):
        for kind in range(2, 4):
            ring_copy(axis, kind).wait()

    def face_target(axis, step):
        a, c = step // 2 // SIDE, step // 2 % SIDE
        to = moved(moved(place, (axis + 1) % 3, a), (axis + 2) % 3, c)
        return to, (core + step) % 2

    def face_index(axis):
        return (place[(axis + 1) % 3] * SIDE + place[(axis + 2) % 3]) * 2 + core

    def pack_into(ref, slot, axis, to):
        for w in range(SIDE):
            pair = want[to, 0, flat_id(put_at(place, axis, w), core)]
            ref[slot, w, 0] = rings[axis][w, pair % 256]
            ref[slot, w, 1] = rings[axis][w, pair // 256]

    def pack(step):
        for axis in range(3):
            to, to_core = face_target(axis, step)
            pack_into(sends[axis], step, axis, flat_id(to, to_core))

    def parcel(axis, step):
        to, to_core = face_target(axis, step)
        return remote(
            sends[axis].at[step], recvs[axis].at[face_index(axis)],
            tile_sems.at[0, axis, step], tile_sems.at[1, axis, step], mesh_id(to, to_core),
        )

    def ship(step, carry):
        pack(step + 1)
        for axis in range(3):
            parcel(axis, step).start()
        return carry

    pack(1)
    lax.fori_loop(1, FACE // 4, ship, 0)
    for k in range(1, n_blk):
        gram_second(k).wait()
    part = gram_t[0]
    for k in range(1, n_blk):
        part = part + gram_b[k]
    gram_t[1] = part
    gram_c[g] = part
    lax.fori_loop(FACE // 4, FACE - 1, ship, 0)
    for axis in range(3):
        parcel(axis, FACE - 1).start()
    for k in range(1, n_grp):
        gram_third(k).start()
    for axis in range(3):
        pack_into(recvs[axis], face_index(axis), axis, me)

    def link(p, state):
        seen, order, last, before = state
        owner = wanted_tiles[p] // held
        hit = lane == owner
        turn = jnp.sum(jnp.where(hit, seen, 0), axis=1, keepdims=True)
        order = jnp.where(lane == p, owner * 2 + jnp.minimum(turn, 1), order)
        seen = jnp.where(hit, 1, seen)
        mine = lane == user_tiles[p]
        earlier = jnp.sum(jnp.where(mine, last, 0), axis=1, keepdims=True)
        before = jnp.where(lane == p, earlier, before)
        last = jnp.where(mine, p + 1, last)
        return seen, order, last, before

    _, order, last, before = lax.fori_loop(0, pairs, link, (zero,) * 4)
    row = lax.broadcasted_iota(jnp.int32, (8, 128), 0)
    table[...] = jnp.where(
        row == 0, order, jnp.where(row == 1, before, jnp.where(row == 2, last, 0))
    )
    table_copy = pltpu.make_async_copy(table, table_s, local_sems.at[2])
    table_copy.start()
    count_copy.wait()

    def weigh(p, carry):
        weights[p] = (counted[p].astype(jnp.float32) * ALPHA).astype(jnp.bfloat16)
        return carry

    lax.fori_loop(0, pairs, weigh, 0)
    chain[0] = jnp.zeros((tile, rank), jnp.float32)
    table_copy.wait()

    gather_end()
    for k in range(1, n_grp):
        gram_third(k).wait()

    def wait_parcel(step, carry):
        for axis in range(3):
            parcel(axis, step).wait()
        return carry

    lax.fori_loop(1, FACE, wait_parcel, 0)

    def take(p, carry):
        slot = table_s[0, p]
        owner, turn = slot // 2, slot % 2
        ob, og = owner // n_grp, owner % n_grp
        at, of = (og // SIDE, og % SIDE, ob // 2), ob % 2
        for axis, (start, rows) in enumerate(SHARE):
            face = (at[(axis + 1) % 3] * SIDE + at[(axis + 2) % 3]) * 2 + of
            tiles[p, start:start + rows] = recvs[axis][face, at[axis], turn]
        return carry

    lax.fori_loop(0, pairs, take, 0)

    def accumulate(with_rhs):
        group = 4

        def several(i, carry):
            backs = []
            for j in range(group):
                p = i * group + j
                factors = tiles[p]
                weight = weights[p].astype(jnp.float32)
                scores = lax.dot_general(
                    low[tile_place(user_tiles[p])], factors, (((1,), (1,)), ((), ())),
                    preferred_element_type=jnp.float32,
                )
                scaled = (weight * scores).astype(jnp.bfloat16)
                back = jnp.dot(scaled, factors, preferred_element_type=jnp.float32)
                if with_rhs:
                    confidence = jnp.where(weight > 0, 1.0 + weight, 0.0).astype(jnp.bfloat16)
                    back = jnp.dot(
                        confidence, factors, preferred_element_type=jnp.float32
                    ) - back
                backs.append(back)
            for j in range(group):
                p = i * group + j
                chain[p + 1] = chain[table_s[1, p]] + backs[j]
            return carry

        lax.fori_loop(0, pairs // group, several, 0)

    near, far = (y, x), (x, y)

    def partial(t, away, end):
        u = 2 * (end * SIDE + away) if t == 0 else 2 * (away * SIDE + end) + 1
        return chain[table_s[2, u]]

    def sum_first(t, k, m):
        to = mesh_id(moved(place, 1 - t, k), core)
        return [
            remote(
                src.at[t, k, m], dst.at[t, k, m], first_sems.at[0, i, t, k, m],
                first_sems.at[1, i, t, k, m], to,
            )
            for i, (src, dst) in enumerate(((part_u, first_u), (part_q, first_q)))
        ]

    def sum_second(t, m):
        to = mesh_id(moved(place, t, m), core)
        return [
            remote(
                src.at[t, m], dst.at[t, m], second_sems.at[0, i, t, m],
                second_sems.at[1, i, t, m], to,
            )
            for i, (src, dst) in enumerate(((sum_u, second_u), (sum_q, second_q)))
        ]

    turns = tuple(range(1, SIDE)) + (0,)

    def reduce_start():
        for m in turns:
            for k in range(1, SIDE):
                for t in range(2):
                    whole, unit = quantize(
                        partial(t, (near[t] + k) % SIDE, (far[t] + m) % SIDE)
                    )
                    part_q[t, k, m] = whole
                    part_u[t, k, m] = unit
                    for copy in sum_first(t, k, m):
                        copy.start()

    def reduce_finish():
        for m in turns:
            for t in range(2):
                total = partial(t, near[t], (far[t] + m) % SIDE)
                for k in range(1, SIDE):
                    for copy in sum_first(t, k, m):
                        copy.wait()
                    total = total + restore(first_q[t, k, m], first_u[t, k, m])
                if m == 0:
                    sums[t] = total
                else:
                    whole, unit = quantize(total)
                    sum_q[t, m] = whole
                    sum_u[t, m] = unit
                    for copy in sum_second(t, m):
                        copy.start()
        totals = []
        for t in range(2):
            total = sums[t]
            for m in range(1, SIDE):
                for copy in sum_second(t, m):
                    copy.wait()
                total = total + restore(second_q[t, m], second_u[t, m])
            totals.append(total)
        return jnp.concatenate(totals, axis=0)

    def gram_term(vectors):
        return (
            jnp.dot(vectors, gram_c[...].reshape(rank, rank), precision=lax.Precision.HIGHEST,
                    preferred_element_type=jnp.float32)
            + REG * vectors
        )

    def row_sum(left, right):
        return jnp.sum(left * right, axis=1, keepdims=True)

    accumulate(True)
    reduce_start()
    local[...] = gram_term(prior[...])
    start = reduce_finish() - local[...]
    residual[...] = start
    direction[...] = start
    out[...] = prior[...]

    def iterate(step, norm_now):
        d_low = direction[...].astype(jnp.bfloat16)
        low[y * SIDE + x] = d_low[:tile]
        low[PLANE + x * SIDE + y] = d_low[tile:]
        gather_begin()
        local[...] = gram_term(direction[...])
        gather_onward()
        gather_end()
        accumulate(False)
        reduce_start()
        image = local[...] + reduce_finish()
        d = direction[...]
        alpha = norm_now / (row_sum(d, image) + EPS)
        out[...] = out[...] + alpha * d
        r = residual[...] - alpha * image
        residual[...] = r
        fresh = row_sum(r, r)
        direction[...] = r + fresh / (norm_now + EPS) * d
        return fresh

    lax.fori_loop(0, ITERS, iterate, row_sum(start, start))


def body(user_prior, item_factors, user_tiles, item_tiles, counts):
    n_blk = lax.axis_size("blk")
    n_grp = lax.axis_size("grp")
    n_all = n_blk * n_grp
    pairs, tile, _ = counts.shape
    rank = item_factors.shape[1]
    users = 2 * n_grp
    own = user_prior.shape[0]
    held = item_factors.shape[0] // tile
    grows = rank // n_grp
    vmem = pl.BlockSpec(memory_space=pltpu.VMEM)
    smem = pl.BlockSpec(memory_space=pltpu.SMEM)
    dma = pltpu.SemaphoreType.DMA
    low_type, whole_type, full = jnp.bfloat16, jnp.int16, jnp.float32
    return pl.pallas_call(
        functools.partial(kernel, n_blk, n_grp),
        out_shape=jax.ShapeDtypeStruct((own, rank), full),
        in_specs=[smem, smem, vmem, vmem, pl.BlockSpec(memory_space=pl.ANY)],
        out_specs=vmem,
        scratch_shapes=[
            pltpu.VMEM((1, 128), jnp.int32),
            pltpu.VMEM((n_all, 1, 128), jnp.int32),
            pltpu.SMEM((n_all, 1, 128), jnp.int32),
            pltpu.VMEM((8, 128), jnp.int32),
            pltpu.SMEM((8, 128), jnp.int32),
            *(pltpu.VMEM((SIDE, held, rows, rank), low_type) for _, rows in SHARE),
            *(pltpu.VMEM((FACE, SIDE, 2, rows, rank), low_type) for _, rows in SHARE),
            *(pltpu.VMEM((FACE, SIDE, 2, rows, rank), low_type) for _, rows in SHARE),
            pltpu.VMEM((pairs, tile, rank), low_type),
            pltpu.VMEM((pairs, tile, tile), jnp.int32),
            pltpu.VMEM((pairs, tile, tile), low_type),
            pltpu.VMEM((users, tile, rank), low_type),
            pltpu.VMEM((pairs + 1, tile, rank), full),
            pltpu.VMEM((n_grp, grows, rank), full),
            pltpu.VMEM((n_grp, grows, rank), full),
            pltpu.VMEM((n_blk, grows, rank), full),
            pltpu.VMEM((n_grp, grows, rank), full),
            pltpu.VMEM((2, grows, rank), full),
            pltpu.VMEM((2, SIDE, SIDE, tile, rank), whole_type),
            pltpu.VMEM((2, SIDE, SIDE, 1, rank), full),
            pltpu.VMEM((2, SIDE, SIDE, tile, rank), whole_type),
            pltpu.VMEM((2, SIDE, SIDE, 1, rank), full),
            pltpu.VMEM((2, SIDE, tile, rank), whole_type),
            pltpu.VMEM((2, SIDE, 1, rank), full),
            pltpu.VMEM((2, SIDE, tile, rank), whole_type),
            pltpu.VMEM((2, SIDE, 1, rank), full),
            pltpu.VMEM((2, tile, rank), full),
            pltpu.VMEM((own, rank), full),
            pltpu.VMEM((own, rank), full),
            pltpu.VMEM((own, rank), full),
            dma((2, n_all)),
            dma((2, 3, 4)),
            dma((2, 3, FACE)),
            dma((2, 2, SIDE)),
            dma((2, 2, SIDE, SIDE)),
            dma((2, 2, 2, SIDE, SIDE)),
            dma((2, 2, 2, SIDE)),
            dma((3, 2, n_grp)),
            dma((3,)),
        ],
        compiler_params=pltpu.CompilerParams(
            collective_id=0, has_side_effects=True, vmem_limit_bytes=60 << 20
        ),
        name="als",
    )(item_tiles, user_tiles, item_factors.reshape(held, tile, rank), user_prior, counts)


def solution(mesh):
    in_specs = (
        P(("blk", "grp"), None),
        P(("blk", "grp"), None),
        P(("blk", "grp")),
        P(("blk", "grp")),
        P(("blk", "grp"), None, None),
    )
    out_specs = P(("blk", "grp"), None)
    return jax.shard_map(body, mesh=mesh, in_specs=in_specs, out_specs=out_specs, check_vma=False)
```

```python
import functools

import jax
import jax.numpy as jnp
from jax import lax
from jax.experimental import pallas as pl
from jax.experimental.pallas import tpu as pltpu
from jax.sharding import PartitionSpec as P

ITERS = 3
ALPHA = 40.0
REG = 32.0
EPS = 1e-06
SIDE = 4
PLANE = SIDE * SIDE
FACE = 2 * PLANE
LEVELS = 32700.0
SHARE = ((0, 48), (48, 48), (96, 32))
AROUND = (0, 1, 3, 2)
CLOSE = 3
SHIFTS = (1, 3, 4, 12, 2, 8, 5, 7, 13, 15, 6, 9, 11, 14, 10)
MESH = pl.DeviceIdType.MESH


def position():
    b = lax.axis_index("blk")
    g = lax.axis_index("grp")
    return (g // SIDE, g % SIDE, b // 2), b % 2


def mesh_id(place, core):
    x, y, z = place
    return z * 2 + core, x * SIDE + y


def flat_id(place, core):
    b, g = mesh_id(place, core)
    return b * PLANE + g


def moved(place, axis, k):
    return tuple((v + k) % SIDE if i == axis else v for i, v in enumerate(place))


def put_at(place, axis, value):
    return tuple(value if i == axis else v for i, v in enumerate(place))


def remote(src, dst, send_sem, recv_sem, device):
    return pltpu.make_async_remote_copy(
        src_ref=src, dst_ref=dst, send_sem=send_sem, recv_sem=recv_sem,
        device_id=device, device_id_type=MESH,
    )


def quantize(value):
    top = jnp.maximum(jnp.max(jnp.abs(value), axis=0, keepdims=True), 1e-30)
    whole = jnp.round(value * (LEVELS / top)).astype(jnp.int32).astype(jnp.int16)
    return whole, top * (1.0 / LEVELS)


def restore(whole, unit):
    return whole.astype(jnp.int32).astype(jnp.float32) * unit


def tile_place(u):
    g = u // 2
    x, y = g // SIDE, g % SIDE
    return jnp.where(u % 2 == 0, y * SIDE + x, PLANE + x * SIDE + y)


def kernel(
    n_blk, n_grp,
    wanted_tiles, user_tiles, items, prior, counts,
    out,
    req, reqs, want, table, table_s,
    ring0, ring1, ring2, far0, far1, far2, send0, send1, send2, recv0, recv1, recv2,
    tiles, counted, weights, pulls, scaled, low, chain,
    gram_own, gram_a, gram_b, gram_c, gram_t,
    part_q, part_u, first_q, first_u, sum_q, sum_u, second_q, second_u, sums,
    residual, direction, local,
    req_sems, ring_sems, tile_sems, gather_one, gather_two, first_sems, second_sems,
    gram_sems, local_sems,
):
    n_all = n_blk * n_grp
    place, core = position()
    x, y, z = place
    b, g = mesh_id(place, core)
    me = b * n_grp + g
    pairs, tile, rank = tiles.shape
    held = items.shape[0]
    fars = (far0, far1, far2)
    rings, sends, recvs = (ring0, ring1, ring2), (send0, send1, send2), (recv0, recv1, recv2)

    count_copy = pltpu.make_async_copy(counts, counted, local_sems.at[0])
    count_copy.start()

    def other(step):
        b_to = (b + step // n_grp) % n_blk
        return b_to, (g + step % n_grp) % n_grp

    barrier = pltpu.get_barrier_semaphore()

    def greet(step, carry):
        pl.semaphore_signal(barrier, inc=1, device_id=other(step), device_id_type=MESH)
        return carry

    lax.fori_loop(1, n_all, greet, 0)

    lane = lax.broadcasted_iota(jnp.int32, (1, 128), 1)
    zero = jnp.zeros((1, 128), jnp.int32)

    def ask(i, state):
        first, second = state
        for j in range(8):
            p = i * 8 + j
            late, early = wanted_tiles[p], wanted_tiles[pairs - 1 - p]
            second = jnp.where(lane == late // held, late % held, second)
            first = jnp.where(lane == early // held, early % held, first)
        return first, second

    first, second = lax.fori_loop(0, pairs // 8, ask, (zero, zero))
    asked = first + 256 * second
    req[...] = asked
    reqs[me] = asked
    low[y * SIDE + x] = prior[:tile].astype(jnp.bfloat16)
    low[PLANE + x * SIDE + y] = prior[tile:].astype(jnp.bfloat16)

    def keep(i, carry):
        for axis, (start, rows) in enumerate(SHARE):
            rings[axis][0, i] = items[i, start:start + rows]
        return carry

    lax.fori_loop(0, held, keep, 0)

    pl.semaphore_wait(barrier, n_all - 1)

    def request(step):
        return remote(
            req, reqs.at[me], req_sems.at[0, step], req_sems.at[1, step], other(step)
        )

    def send_request(step, carry):
        request(step).start()
        return carry

    lax.fori_loop(1, n_all, send_request, 0)

    def ring_copy(axis, kind):
        start, rows = SHARE[axis]
        source = 2 if kind % 2 == 0 else 1
        if kind < 2:
            src, dst = items.at[:, pl.ds(start, rows)], rings[axis].at[source]
        else:
            half = pl.ds(0 if kind == 2 else held // 2, held // 2)
            src, dst = rings[axis].at[source, half], fars[axis].at[half]
        to = moved(place, axis, 1 if kind % 2 == 0 else SIDE - 1)
        return remote(
            src, dst, ring_sems.at[0, axis, kind], ring_sems.at[1, axis, kind],
            mesh_id(to, core),
        )

    for kind in range(2):
        for axis in range(3):
            ring_copy(axis, kind).start()

    def low_place(t, m):
        if t == 0:
            return y * SIDE + (x + SIDE - m) % SIDE
        return PLANE + x * SIDE + (y + SIDE - m) % SIDE

    def gather_a(t, k):
        ref = low.at[low_place(t, 0)]
        return remote(
            ref, ref, gather_one.at[0, t, k], gather_one.at[1, t, k],
            mesh_id(moved(place, t, k), core),
        )

    def gather_b(t, k, m):
        ref = low.at[low_place(t, m)]
        return remote(
            ref, ref, gather_two.at[0, t, k, m], gather_two.at[1, t, k, m],
            mesh_id(moved(place, 1 - t, k), core),
        )

    def gather_begin():
        for k in range(1, SIDE):
            for t in range(2):
                gather_a(t, k).start()
        for k in range(1, SIDE):
            for t in range(2):
                gather_b(t, k, 0).start()

    def gather_onward():
        for m in range(1, SIDE):
            for t in range(2):
                gather_a(t, m).wait()
                for k in range(1, SIDE):
                    gather_b(t, k, m).start()

    def gather_end():
        for m in range(SIDE):
            for k in range(1, SIDE):
                for t in range(2):
                    gather_b(t, k, m).wait()

    gather_begin()

    chunk = min(8, held)

    def gram_step(i, total):
        block = items[pl.ds(i * chunk, chunk)].reshape(chunk * tile, rank)
        return total + lax.dot_general(
            block, block, (((0,), (0,)), ((), ())), preferred_element_type=jnp.float32
        )

    gram_own[...] = lax.fori_loop(
        0, held // chunk, gram_step, jnp.zeros((rank, rank), jnp.float32)
    ).reshape(n_grp, rank // n_grp, rank)

    def gram_first(k):
        to = (g + k) % n_grp
        return remote(
            gram_own.at[to], gram_a.at[k], gram_sems.at[0, 0, k], gram_sems.at[0, 1, k], (b, to)
        )

    def gram_second(k):
        return remote(
            gram_t.at[0], gram_b.at[k], gram_sems.at[1, 0, k], gram_sems.at[1, 1, k],
            ((b + k) % n_blk, g),
        )

    def gram_third(k):
        return remote(
            gram_t.at[1], gram_c.at[g], gram_sems.at[2, 0, k], gram_sems.at[2, 1, k],
            (b, (g + k) % n_grp),
        )

    for k in range(1, n_grp):
        gram_first(k).start()

    for axis in range(3):
        for kind in range(2):
            ring_copy(axis, kind).wait()
            ring_copy(axis, kind + 2).start()

    gather_onward()

    def wait_request(step, carry):
        request(step).wait()
        return carry

    lax.fori_loop(1, n_all, wait_request, 0)
    want_copy = pltpu.make_async_copy(reqs, want, local_sems.at[1])
    want_copy.start()
    for k in range(1, n_grp):
        gram_first(k).wait()
    part = gram_own[g]
    for k in range(1, n_grp):
        part = part + gram_a[k]
    gram_t[0] = part
    want_copy.wait()
    for k in range(1, n_blk):
        gram_second(k).start()

    def face_shift(turn):
        words = [sum(v << 4 * j for j, v in enumerate(SHIFTS[i:i + 7])) for i in (0, 7, 14)]
        i = turn // 2
        word = jnp.where(i < 7, words[0], jnp.where(i < 14, words[1], words[2]))
        shift = lax.shift_right_logical(jnp.int32(word), 4 * (i % 7)) % 16
        return shift * 2 + turn % 2

    def face_target(axis, step):
        a, c = step // 2 // SIDE, step // 2 % SIDE
        to = moved(moved(place, (axis + 1) % 3, a), (axis + 2) % 3, c)
        return to, (core + step) % 2

    def face_index(axis):
        return (place[(axis + 1) % 3] * SIDE + place[(axis + 2) % 3]) * 2 + core

    def pack_into(ref, slot, axis, to, which):
        for i in which:
            w = (place[axis] + AROUND[i]) % SIDE
            pair = want[to, 0, flat_id(put_at(place, axis, w), core)]
            for j, held_at in enumerate((pair % 256, pair // 256)):
                ref[slot, i, j] = rings[axis][i, held_at] if i < CLOSE else fars[axis][held_at]

    levels = (tuple(range(CLOSE)), tuple(range(CLOSE, SIDE)))

    def pack(level, step):
        for axis in range(3):
            to, to_core = face_target(axis, step)
            pack_into(sends[axis], step, axis, flat_id(to, to_core), levels[level])

    def parcel(level, axis, step):
        to, to_core = face_target(axis, step)
        part = pl.ds(levels[level][0], len(levels[level]))
        return remote(
            sends[axis].at[step, part], recvs[axis].at[face_index(axis), part],
            tile_sems.at[0, level, axis, step], tile_sems.at[1, level, axis, step],
            mesh_id(to, to_core),
        )

    def ship(level, first, last):
        pack(level, face_shift(first))

        def one(turn, carry):
            pack(level, face_shift(turn + 1))
            for axis in range(3):
                parcel(level, axis, face_shift(turn)).start()
            return carry

        lax.fori_loop(first, last - 1, one, 0)
        for axis in range(3):
            parcel(level, axis, face_shift(last - 1)).start()

    turns_all = 2 * len(SHIFTS)
    ship(0, 0, 8)
    for k in range(1, n_blk):
        gram_second(k).wait()
    part = gram_t[0]
    for k in range(1, n_blk):
        part = part + gram_b[k]
    gram_t[1] = part
    gram_c[g] = part
    ship(0, 8, turns_all)
    for axis in range(3):
        for kind in range(2, 4):
            ring_copy(axis, kind).wait()
    pack(0, 1)
    pack(1, 1)
    ship(1, 0, turns_all)
    for level in range(2):
        for axis in range(3):
            parcel(level, axis, 1).start()
    for k in range(1, n_grp):
        gram_third(k).start()
    for axis in range(3):
        pack_into(recvs[axis], face_index(axis), axis, me, range(SIDE))

    def link(p, state):
        seen, order, last, before = state
        owner = wanted_tiles[p] // held
        hit = lane == owner
        turn = jnp.sum(jnp.where(hit, seen, 0), axis=1, keepdims=True)
        order = jnp.where(lane == p, owner * 2 + jnp.minimum(turn, 1), order)
        seen = jnp.where(hit, 1, seen)
        mine = lane == user_tiles[p]
        earlier = jnp.sum(jnp.where(mine, last, 0), axis=1, keepdims=True)
        before = jnp.where(lane == p, earlier, before)
        last = jnp.where(mine, p + 1, last)
        return seen, order, last, before

    _, order, last, before = lax.fori_loop(0, pairs, link, (zero,) * 4)
    row = lax.broadcasted_iota(jnp.int32, (8, 128), 0)
    table[...] = jnp.where(
        row == 0, order, jnp.where(row == 1, before, jnp.where(row == 2, last, 0))
    )
    table_copy = pltpu.make_async_copy(table, table_s, local_sems.at[2])
    table_copy.start()
    count_copy.wait()

    def weigh(p, carry):
        weight = counted[p].astype(jnp.float32) * ALPHA
        weights[p] = weight.astype(jnp.bfloat16)
        pulls[p] = jnp.where(weight > 0, 1.0 + weight, 0.0).astype(jnp.bfloat16)
        return carry

    lax.fori_loop(0, pairs, weigh, 0)
    chain[0] = jnp.zeros((tile, rank), jnp.float32)
    table_copy.wait()

    gather_end()
    for k in range(1, n_grp):
        gram_third(k).wait()

    def wait_parcel(step, carry):
        for level in range(2):
            for axis in range(3):
                parcel(level, axis, step).wait()
        return carry

    lax.fori_loop(1, FACE, wait_parcel, 0)

    def take(i, carry):
        for j in range(4):
            p = i * 4 + j
            slot = table_s[0, p]
            owner, turn = slot // 2, slot % 2
            ob, og = owner // n_grp, owner % n_grp
            at, of = (og // SIDE, og % SIDE, ob // 2), ob % 2
            for axis, (start, rows) in enumerate(SHARE):
                face = (at[(axis + 1) % 3] * SIDE + at[(axis + 2) % 3]) * 2 + of
                ahead = (at[axis] + SIDE - place[axis]) % SIDE
                ahead = jnp.where(ahead >= 2, 5 - ahead, ahead)
                tiles[p, start:start + rows] = recvs[axis][face, ahead, turn]
        return carry

    lax.fori_loop(0, pairs // 4, take, 0)

    group = 8

    def accumulate(with_rhs):
        def score(i, carry):
            for j in range(group):
                p = i * group + j
                scores = lax.dot_general(
                    low[tile_place(user_tiles[p])], tiles[p], (((1,), (1,)), ((), ())),
                    preferred_element_type=jnp.float32,
                )
                scaled[p] = (weights[p].astype(jnp.float32) * scores).astype(jnp.bfloat16)
            return carry

        lax.fori_loop(0, pairs // group, score, 0)

        def spread(i, carry):
            backs = []
            for j in range(group):
                p = i * group + j
                back = jnp.dot(scaled[p], tiles[p], preferred_element_type=jnp.float32)
                if with_rhs:
                    pulled = jnp.dot(pulls[p], tiles[p], preferred_element_type=jnp.float32)
                    back = pulled - back
                backs.append(back)
            for j in range(group):
                p = i * group + j
                chain[p + 1] = chain[table_s[1, p]] + backs[j]
            return carry

        lax.fori_loop(0, pairs // group, spread, 0)

    near, far = (y, x), (x, y)

    def partial(t, away, end):
        u = 2 * (end * SIDE + away) if t == 0 else 2 * (away * SIDE + end) + 1
        return chain[table_s[2, u]]

    def sum_first(t, k, m):
        to = mesh_id(moved(place, 1 - t, k), core)
        return [
            remote(
                src.at[t, k, m], dst.at[t, k, m], first_sems.at[0, i, t, k, m],
                first_sems.at[1, i, t, k, m], to,
            )
            for i, (src, dst) in enumerate(((part_u, first_u), (part_q, first_q)))
        ]

    def sum_second(t, m):
        to = mesh_id(moved(place, t, m), core)
        return [
            remote(
                src.at[t, m], dst.at[t, m], second_sems.at[0, i, t, m],
                second_sems.at[1, i, t, m], to,
            )
            for i, (src, dst) in enumerate(((sum_u, second_u), (sum_q, second_q)))
        ]

    turns = tuple(range(1, SIDE)) + (0,)

    def reduce_start():
        for m in turns:
            for k in range(1, SIDE):
                for t in range(2):
                    whole, unit = quantize(
                        partial(t, (near[t] + k) % SIDE, (far[t] + m) % SIDE)
                    )
                    part_q[t, k, m] = whole
                    part_u[t, k, m] = unit
                    for copy in sum_first(t, k, m):
                        copy.start()

    def reduce_finish():
        for m in turns:
            for t in range(2):
                total = partial(t, near[t], (far[t] + m) % SIDE)
                for k in range(1, SIDE):
                    for copy in sum_first(t, k, m):
                        copy.wait()
                    total = total + restore(first_q[t, k, m], first_u[t, k, m])
                if m == 0:
                    sums[t] = total
                else:
                    whole, unit = quantize(total)
                    sum_q[t, m] = whole
                    sum_u[t, m] = unit
                    for copy in sum_second(t, m):
                        copy.start()
        totals = []
        for t in range(2):
            total = sums[t]
            for m in range(1, SIDE):
                for copy in sum_second(t, m):
                    copy.wait()
                total = total + restore(second_q[t, m], second_u[t, m])
            totals.append(total)
        return jnp.concatenate(totals, axis=0)

    def gram_term(vectors):
        return (
            jnp.dot(vectors, gram_c[...].reshape(rank, rank), precision=lax.Precision.HIGHEST,
                    preferred_element_type=jnp.float32)
            + REG * vectors
        )

    def row_sum(left, right):
        return jnp.sum(left * right, axis=1, keepdims=True)

    accumulate(True)
    reduce_start()
    local[...] = gram_term(prior[...])
    start = reduce_finish() - local[...]
    residual[...] = start
    direction[...] = start
    out[...] = prior[...]

    def iterate(step, norm_now):
        d_low = direction[...].astype(jnp.bfloat16)
        low[y * SIDE + x] = d_low[:tile]
        low[PLANE + x * SIDE + y] = d_low[tile:]
        gather_begin()
        local[...] = gram_term(direction[...])
        gather_onward()
        gather_end()
        accumulate(False)
        reduce_start()
        image = local[...] + reduce_finish()
        d = direction[...]
        alpha = norm_now / (row_sum(d, image) + EPS)
        out[...] = out[...] + alpha * d
        r = residual[...] - alpha * image
        residual[...] = r
        fresh = row_sum(r, r)
        direction[...] = r + fresh / (norm_now + EPS) * d
        return fresh

    lax.fori_loop(0, ITERS, iterate, row_sum(start, start))


def body(user_prior, item_factors, user_tiles, item_tiles, counts):
    n_blk = lax.axis_size("blk")
    n_grp = lax.axis_size("grp")
    n_all = n_blk * n_grp
    pairs, tile, _ = counts.shape
    rank = item_factors.shape[1]
    users = 2 * n_grp
    own = user_prior.shape[0]
    held = item_factors.shape[0] // tile
    grows = rank // n_grp
    vmem = pl.BlockSpec(memory_space=pltpu.VMEM)
    smem = pl.BlockSpec(memory_space=pltpu.SMEM)
    dma = pltpu.SemaphoreType.DMA
    low_type, whole_type, full = jnp.bfloat16, jnp.int16, jnp.float32
    return pl.pallas_call(
        functools.partial(kernel, n_blk, n_grp),
        out_shape=jax.ShapeDtypeStruct((own, rank), full),
        in_specs=[smem, smem, vmem, vmem, pl.BlockSpec(memory_space=pl.ANY)],
        out_specs=vmem,
        scratch_shapes=[
            pltpu.VMEM((1, 128), jnp.int32),
            pltpu.VMEM((n_all, 1, 128), jnp.int32),
            pltpu.SMEM((n_all, 1, 128), jnp.int32),
            pltpu.VMEM((8, 128), jnp.int32),
            pltpu.SMEM((8, 128), jnp.int32),
            *(pltpu.VMEM((CLOSE, held, rows, rank), low_type) for _, rows in SHARE),
            *(pltpu.VMEM((held, rows, rank), low_type) for _, rows in SHARE),
            *(pltpu.VMEM((FACE, SIDE, 2, rows, rank), low_type) for _, rows in SHARE),
            *(pltpu.VMEM((FACE, SIDE, 2, rows, rank), low_type) for _, rows in SHARE),
            pltpu.VMEM((pairs, tile, rank), low_type),
            pltpu.VMEM((pairs, tile, tile), jnp.int32),
            pltpu.VMEM((pairs, tile, tile), low_type),
            pltpu.VMEM((pairs, tile, tile), low_type),
            pltpu.VMEM((pairs, tile, tile), low_type),
            pltpu.VMEM((users, tile, rank), low_type),
            pltpu.VMEM((pairs + 1, tile, rank), full),
            pltpu.VMEM((n_grp, grows, rank), full),
            pltpu.VMEM((n_grp, grows, rank), full),
            pltpu.VMEM((n_blk, grows, rank), full),
            pltpu.VMEM((n_grp, grows, rank), full),
            pltpu.VMEM((2, grows, rank), full),
            pltpu.VMEM((2, SIDE, SIDE, tile, rank), whole_type),
            pltpu.VMEM((2, SIDE, SIDE, 1, rank), full),
            pltpu.VMEM((2, SIDE, SIDE, tile, rank), whole_type),
            pltpu.VMEM((2, SIDE, SIDE, 1, rank), full),
            pltpu.VMEM((2, SIDE, tile, rank), whole_type),
            pltpu.VMEM((2, SIDE, 1, rank), full),
            pltpu.VMEM((2, SIDE, tile, rank), whole_type),
            pltpu.VMEM((2, SIDE, 1, rank), full),
            pltpu.VMEM((2, tile, rank), full),
            pltpu.VMEM((own, rank), full),
            pltpu.VMEM((own, rank), full),
            pltpu.VMEM((own, rank), full),
            dma((2, n_all)),
            dma((2, 3, 4)),
            dma((2, 2, 3, FACE)),
            dma((2, 2, SIDE)),
            dma((2, 2, SIDE, SIDE)),
            dma((2, 2, 2, SIDE, SIDE)),
            dma((2, 2, 2, SIDE)),
            dma((3, 2, n_grp)),
            dma((3,)),
        ],
        compiler_params=pltpu.CompilerParams(
            collective_id=0, has_side_effects=True, vmem_limit_bytes=60 << 20
        ),
        name="als",
    )(item_tiles, user_tiles, item_factors.reshape(held, tile, rank), user_prior, counts)


def solution(mesh):
    in_specs = (
        P(("blk", "grp"), None),
        P(("blk", "grp"), None),
        P(("blk", "grp")),
        P(("blk", "grp")),
        P(("blk", "grp"), None, None),
    )
    out_specs = P(("blk", "grp"), None)
    return jax.shard_map(body, mesh=mesh, in_specs=in_specs, out_specs=out_specs, check_vma=False)
```

```python
import functools

import jax
import jax.numpy as jnp
from jax import lax
from jax.experimental import pallas as pl
from jax.experimental.pallas import tpu as pltpu
from jax.sharding import PartitionSpec as P

ITERS = 3
ALPHA = 40.0
REG = 32.0
EPS = 1e-06
SIDE = 4
PLANE = SIDE * SIDE
FACE = 2 * PLANE
PEERS = 73
LEVELS = 32700.0
SHARE = ((0, 48), (48, 48), (96, 32))
AROUND = (0, 1, 3, 2)
CLOSE = 3
SHIFTS = (1, 3, 4, 12, 2, 8, 5, 15, 7, 13, 6, 14, 9, 11, 10)
MESH = pl.DeviceIdType.MESH


def position():
    b = lax.axis_index("blk")
    g = lax.axis_index("grp")
    return (g // SIDE, g % SIDE, b // 2), b % 2


def mesh_id(place, core):
    x, y, z = place
    return z * 2 + core, x * SIDE + y


def flat_id(place, core):
    b, g = mesh_id(place, core)
    return b * PLANE + g


def moved(place, axis, k):
    return tuple((v + k) % SIDE if i == axis else v for i, v in enumerate(place))


def put_at(place, axis, value):
    return tuple(value if i == axis else v for i, v in enumerate(place))


def remote(src, dst, send_sem, recv_sem, device):
    return pltpu.make_async_remote_copy(
        src_ref=src, dst_ref=dst, send_sem=send_sem, recv_sem=recv_sem,
        device_id=device, device_id_type=MESH,
    )


def quantize(value):
    top = jnp.maximum(jnp.max(jnp.abs(value), axis=0, keepdims=True), 1e-30)
    whole = jnp.round(value * (LEVELS / top)).astype(jnp.int32).astype(jnp.int16)
    return whole, top * (1.0 / LEVELS)


def restore(whole, unit):
    return whole.astype(jnp.int32).astype(jnp.float32) * unit


def tile_place(u):
    g = u // 2
    x, y = g // SIDE, g % SIDE
    return jnp.where(u % 2 == 0, y * SIDE + x, PLANE + x * SIDE + y)


def kernel(
    n_blk, n_grp,
    wanted_tiles, user_tiles, items, prior, counts,
    out,
    req, reqs, want, table, table_s,
    ring0, ring1, ring2, far0, far1, far2, send0, send1, send2, recv0, recv1, recv2,
    tiles, counted, weights, pulls, scaled, low0, low1, chain,
    gram_own, gram_a, gram_b, gram_c, gram_t,
    part_q, part_u, first_q, first_u, sum_q, sum_u, second_q, second_u, sums,
    residual, direction, local,
    req_sems, ring_sems, tile_sems, gather_one, gather_two, first_sems, second_sems,
    gram_sems, local_sems,
):
    n_all = n_blk * n_grp
    place, core = position()
    x, y, z = place
    b, g = mesh_id(place, core)
    me = b * n_grp + g
    pairs, tile, rank = tiles.shape
    held = items.shape[0]
    half = tile // 2
    fars = (far0, far1, far2)
    lows = (low0, low1)
    rings, sends, recvs = (ring0, ring1, ring2), (send0, send1, send2), (recv0, recv1, recv2)

    def half_rows(ref, h):
        return jnp.concatenate(
            [ref[t * tile + h * half:t * tile + (h + 1) * half] for t in range(2)], axis=0
        )

    def lower(h, vectors):
        d_low = vectors.astype(jnp.bfloat16)
        lows[h][y * SIDE + x] = d_low[:half]
        lows[h][PLANE + x * SIDE + y] = d_low[half:]

    count_copy = pltpu.make_async_copy(counts, counted, local_sems.at[0])
    count_copy.start()

    def same_x(i):
        return (place[0], (y + i // 8) % SIDE, (z + i // 2) % SIDE), (core + i) % 2

    def same_y(i):
        return ((x + 1 + i // 8) % SIDE, place[1], (z + i // 2) % SIDE), (core + i) % 2

    def same_z(i):
        return ((x + 1 + i // 2 % 3) % SIDE, (y + 1 + i // 6) % SIDE, place[2]), (core + i) % 2

    families = ((same_x, 1, 32, 0), (same_y, 0, 24, 32), (same_z, 0, 18, 56))

    def for_peers(act):
        for family, first, last, base in families:
            def one(i, carry):
                act(mesh_id(*family(i)), base + i)
                return carry

            lax.fori_loop(first, last, one, 0)

    barrier = pltpu.get_barrier_semaphore()
    for_peers(
        lambda to, i: pl.semaphore_signal(barrier, inc=1, device_id=to, device_id_type=MESH)
    )

    lane = lax.broadcasted_iota(jnp.int32, (1, 128), 1)
    zero = jnp.zeros((1, 128), jnp.int32)

    def ask(i, state):
        first, second = state
        for j in range(8):
            p = i * 8 + j
            late, early = wanted_tiles[p], wanted_tiles[pairs - 1 - p]
            second = jnp.where(lane == late // held, late % held, second)
            first = jnp.where(lane == early // held, early % held, first)
        return first, second

    first, second = lax.fori_loop(0, pairs // 8, ask, (zero, zero))
    asked = first + 256 * second
    req[...] = asked
    reqs[me] = asked
    for h in range(2):
        lower(h, half_rows(prior, h))

    def keep(i, carry):
        for axis, (start, rows) in enumerate(SHARE):
            rings[axis][0, i] = items[i, start:start + rows]
        return carry

    lax.fori_loop(0, held, keep, 0)

    pl.semaphore_wait(barrier, PEERS)

    def request(to, i):
        return remote(req, reqs.at[me], req_sems.at[0, i], req_sems.at[1, i], to)

    for_peers(lambda to, i: request(to, i).start())

    def ring_copy(axis, kind):
        start, rows = SHARE[axis]
        source = 2 if kind % 2 == 0 else 1
        if kind < 2:
            src, dst = items.at[:, pl.ds(start, rows)], rings[axis].at[source]
        else:
            half = pl.ds(0 if kind == 2 else held // 2, held // 2)
            src, dst = rings[axis].at[source, half], fars[axis].at[half]
        to = moved(place, axis, 1 if kind % 2 == 0 else SIDE - 1)
        return remote(
            src, dst, ring_sems.at[0, axis, kind], ring_sems.at[1, axis, kind],
            mesh_id(to, core),
        )

    for kind in range(2):
        for axis in range(3):
            ring_copy(axis, kind).start()

    def low_place(t, m):
        if t == 0:
            return y * SIDE + (x + SIDE - m) % SIDE
        return PLANE + x * SIDE + (y + SIDE - m) % SIDE

    def gather_a(h, t, k):
        ref = lows[h].at[low_place(t, 0)]
        return remote(
            ref, ref, gather_one.at[0, h, t, k], gather_one.at[1, h, t, k],
            mesh_id(moved(place, t, k), core),
        )

    def gather_b(h, t, k, m):
        ref = lows[h].at[low_place(t, m)]
        return remote(
            ref, ref, gather_two.at[0, h, t, k, m], gather_two.at[1, h, t, k, m],
            mesh_id(moved(place, 1 - t, k), core),
        )

    def gather_begin(h):
        for k in range(1, SIDE):
            for t in range(2):
                gather_a(h, t, k).start()
        for k in range(1, SIDE):
            for t in range(2):
                gather_b(h, t, k, 0).start()

    def gather_onward(h):
        for m in range(1, SIDE):
            for t in range(2):
                gather_a(h, t, m).wait()
                for k in range(1, SIDE):
                    gather_b(h, t, k, m).start()

    def gather_end(h):
        for m in range(SIDE):
            for k in range(1, SIDE):
                for t in range(2):
                    gather_b(h, t, k, m).wait()

    gather_begin(0)
    gather_begin(1)

    chunk = min(8, held)

    def gram_step(i, total):
        block = items[pl.ds(i * chunk, chunk)].reshape(chunk * tile, rank)
        return total + lax.dot_general(
            block, block, (((0,), (0,)), ((), ())), preferred_element_type=jnp.float32
        )

    gram_own[...] = lax.fori_loop(
        0, held // chunk, gram_step, jnp.zeros((rank, rank), jnp.float32)
    ).reshape(n_grp, rank // n_grp, rank)

    def gram_first(k):
        to = (g + k) % n_grp
        return remote(
            gram_own.at[to], gram_a.at[k], gram_sems.at[0, 0, k], gram_sems.at[0, 1, k], (b, to)
        )

    def gram_second(k):
        return remote(
            gram_t.at[0], gram_b.at[k], gram_sems.at[1, 0, k], gram_sems.at[1, 1, k],
            ((b + k) % n_blk, g),
        )

    def gram_third(k):
        return remote(
            gram_t.at[1], gram_c.at[g], gram_sems.at[2, 0, k], gram_sems.at[2, 1, k],
            (b, (g + k) % n_grp),
        )

    for k in range(1, n_grp):
        gram_first(k).start()

    for_peers(lambda to, i: request(to, i).wait())
    want_copy = pltpu.make_async_copy(reqs, want, local_sems.at[1])
    want_copy.start()
    for axis in range(3):
        for kind in range(2):
            ring_copy(axis, kind).wait()
            ring_copy(axis, kind + 2).start()
    want_copy.wait()

    def face_shift(turn):
        words = [sum(v << 4 * j for j, v in enumerate(SHIFTS[i:i + 7])) for i in (0, 7, 14)]
        last = turn >= 28
        i = jnp.where(last, 14, turn // 4 * 2 + turn % 2)
        flip = jnp.where(last, turn % 2, turn // 2 % 2)
        word = jnp.where(i < 7, words[0], jnp.where(i < 14, words[1], words[2]))
        shift = lax.shift_right_logical(jnp.int32(word), 4 * (i % 7)) % 16
        return shift * 2 + flip

    def face_target(axis, step):
        a, c = step // 2 // SIDE, step // 2 % SIDE
        a = jnp.where(core == 0, a, (SIDE - a) % SIDE)
        c = jnp.where(core == 0, c, (SIDE - c) % SIDE)
        to = moved(moved(place, (axis + 1) % 3, a), (axis + 2) % 3, c)
        return to, (core + step) % 2

    def face_index(axis):
        return (place[(axis + 1) % 3] * SIDE + place[(axis + 2) % 3]) * 2 + core

    def pack_into(ref, slot, axis, to, which):
        for i in which:
            w = (place[axis] + AROUND[i]) % SIDE
            pair = want[to, 0, flat_id(put_at(place, axis, w), core)]
            for j, held_at in enumerate((pair % 256, pair // 256)):
                ref[slot, i, j] = rings[axis][i, held_at] if i < CLOSE else fars[axis][held_at]

    levels = (tuple(range(CLOSE)), tuple(range(CLOSE, SIDE)))

    def pack(level, step):
        for axis in range(3):
            to, to_core = face_target(axis, step)
            pack_into(sends[axis], step, axis, flat_id(to, to_core), levels[level])

    def parcel(level, axis, step):
        to, to_core = face_target(axis, step)
        part = pl.ds(levels[level][0], len(levels[level]))
        return remote(
            sends[axis].at[step, part], recvs[axis].at[face_index(axis), part],
            tile_sems.at[0, level, axis, step], tile_sems.at[1, level, axis, step],
            mesh_id(to, to_core),
        )

    def ship(level, first, last):
        pack(level, face_shift(first))

        def one(turn, carry):
            pack(level, face_shift(turn + 1))
            for axis in range(3):
                parcel(level, axis, face_shift(turn)).start()
            return carry

        lax.fori_loop(first, last - 1, one, 0)
        for axis in range(3):
            parcel(level, axis, face_shift(last - 1)).start()

    turns_all = 2 * len(SHIFTS)
    ship(0, 0, 4)
    gather_onward(0)
    gather_onward(1)
    for k in range(1, n_grp):
        gram_first(k).wait()
    part = gram_own[g]
    for k in range(1, n_grp):
        part = part + gram_a[k]
    gram_t[0] = part
    ship(0, 4, 16)
    for k in range(1, n_blk):
        gram_second(k).start()
    ship(0, 16, turns_all)
    for k in range(1, n_blk):
        gram_second(k).wait()
    part = gram_t[0]
    for k in range(1, n_blk):
        part = part + gram_b[k]
    gram_t[1] = part
    gram_c[g] = part
    for axis in range(3):
        for kind in range(2, 4):
            ring_copy(axis, kind).wait()
    pack(0, 1)
    pack(1, 1)
    ship(1, 0, turns_all)
    for level in range(2):
        for axis in range(3):
            parcel(level, axis, 1).start()
    for k in range(1, n_grp):
        gram_third(k).start()
    for axis in range(3):
        pack_into(recvs[axis], face_index(axis), axis, me, range(SIDE))

    def link(p, state):
        seen, order, last, before = state
        owner = wanted_tiles[p] // held
        hit = lane == owner
        turn = jnp.sum(jnp.where(hit, seen, 0), axis=1, keepdims=True)
        order = jnp.where(lane == p, owner * 2 + jnp.minimum(turn, 1), order)
        seen = jnp.where(hit, 1, seen)
        mine = lane == user_tiles[p]
        earlier = jnp.sum(jnp.where(mine, last, 0), axis=1, keepdims=True)
        before = jnp.where(lane == p, earlier, before)
        last = jnp.where(mine, p + 1, last)
        return seen, order, last, before

    _, order, last, before = lax.fori_loop(0, pairs, link, (zero,) * 4)
    row = lax.broadcasted_iota(jnp.int32, (8, 128), 0)
    table[...] = jnp.where(
        row == 0, order, jnp.where(row == 1, before, jnp.where(row == 2, last, 0))
    )
    table_copy = pltpu.make_async_copy(table, table_s, local_sems.at[2])
    table_copy.start()
    count_copy.wait()

    def weigh(p, carry):
        weight = counted[p].astype(jnp.float32) * ALPHA
        weights[p] = weight.astype(jnp.bfloat16)
        pulls[p] = jnp.where(weight > 0, 1.0 + weight, 0.0).astype(jnp.bfloat16)
        return carry

    lax.fori_loop(0, pairs, weigh, 0)
    for h in range(2):
        chain[h, 0] = jnp.zeros((half, rank), jnp.float32)
    table_copy.wait()

    gather_end(0)
    gather_end(1)
    for k in range(1, n_grp):
        gram_third(k).wait()

    def wait_parcel(step, carry):
        for level in range(2):
            for axis in range(3):
                parcel(level, axis, step).wait()
        return carry

    lax.fori_loop(1, FACE, wait_parcel, 0)

    def take(i, carry):
        for j in range(4):
            p = i * 4 + j
            slot = table_s[0, p]
            owner, turn = slot // 2, slot % 2
            ob, og = owner // n_grp, owner % n_grp
            at, of = (og // SIDE, og % SIDE, ob // 2), ob % 2
            for axis, (start, rows) in enumerate(SHARE):
                face = (at[(axis + 1) % 3] * SIDE + at[(axis + 2) % 3]) * 2 + of
                ahead = (at[axis] + SIDE - place[axis]) % SIDE
                ahead = jnp.where(ahead >= 2, 5 - ahead, ahead)
                tiles[p, start:start + rows] = recvs[axis][face, ahead, turn]
        return carry

    lax.fori_loop(0, pairs // 4, take, 0)

    group = 8

    def accumulate(h, with_rhs):
        part = slice(h * half, (h + 1) * half)

        def score(i, carry):
            for j in range(group):
                p = i * group + j
                scores = lax.dot_general(
                    lows[h][tile_place(user_tiles[p])], tiles[p], (((1,), (1,)), ((), ())),
                    preferred_element_type=jnp.float32,
                )
                scaled[p] = (weights[p, part].astype(jnp.float32) * scores).astype(jnp.bfloat16)
            return carry

        lax.fori_loop(0, pairs // group, score, 0)

        def spread(i, carry):
            backs = []
            for j in range(group):
                p = i * group + j
                back = jnp.dot(scaled[p], tiles[p], preferred_element_type=jnp.float32)
                if with_rhs:
                    pulled = jnp.dot(
                        pulls[p, part], tiles[p], preferred_element_type=jnp.float32
                    )
                    back = pulled - back
                backs.append(back)
            for j in range(group):
                p = i * group + j
                chain[h, p + 1] = chain[h, table_s[1, p]] + backs[j]
            return carry

        lax.fori_loop(0, pairs // group, spread, 0)

    near, far = (y, x), (x, y)

    def partial(h, t, away, end):
        u = 2 * (end * SIDE + away) if t == 0 else 2 * (away * SIDE + end) + 1
        return chain[h, table_s[2, u]]

    def sum_first(h, t, k, m):
        to = mesh_id(moved(place, 1 - t, k), core)
        return [
            remote(
                src.at[h, t, k, m], dst.at[h, t, k, m], first_sems.at[0, i, h, t, k, m],
                first_sems.at[1, i, h, t, k, m], to,
            )
            for i, (src, dst) in enumerate(((part_u, first_u), (part_q, first_q)))
        ]

    def sum_second(h, t, m):
        to = mesh_id(moved(place, t, m), core)
        return [
            remote(
                src.at[h, t, m], dst.at[h, t, m], second_sems.at[0, i, h, t, m],
                second_sems.at[1, i, h, t, m], to,
            )
            for i, (src, dst) in enumerate(((sum_u, second_u), (sum_q, second_q)))
        ]

    turns = tuple(range(1, SIDE)) + (0,)

    def reduce_begin(h):
        for m in turns:
            for k in range(1, SIDE):
                for t in range(2):
                    whole, unit = quantize(
                        partial(h, t, (near[t] + k) % SIDE, (far[t] + m) % SIDE)
                    )
                    part_q[h, t, k, m] = whole
                    part_u[h, t, k, m] = unit
                    for copy in sum_first(h, t, k, m):
                        copy.start()

    def reduce_onward(h):
        for m in turns:
            for t in range(2):
                total = partial(h, t, near[t], (far[t] + m) % SIDE)
                for k in range(1, SIDE):
                    for copy in sum_first(h, t, k, m):
                        copy.wait()
                    total = total + restore(first_q[h, t, k, m], first_u[h, t, k, m])
                if m == 0:
                    sums[h, t] = total
                else:
                    whole, unit = quantize(total)
                    sum_q[h, t, m] = whole
                    sum_u[h, t, m] = unit
                    for copy in sum_second(h, t, m):
                        copy.start()

    def reduce_end(h):
        totals = []
        for t in range(2):
            total = sums[h, t]
            for m in range(1, SIDE):
                for copy in sum_second(h, t, m):
                    copy.wait()
                total = total + restore(second_q[h, t, m], second_u[h, t, m])
            totals.append(total)
        return jnp.concatenate(totals, axis=0)

    def gram_term(vectors):
        return (
            jnp.dot(vectors, gram_c[...].reshape(rank, rank), precision=lax.Precision.HIGHEST,
                    preferred_element_type=jnp.float32)
            + REG * vectors
        )

    def row_sum(left, right):
        return jnp.sum(left * right, axis=1, keepdims=True)

    norms = []
    out[...] = prior[...]
    for h in range(2):
        accumulate(h, True)
        reduce_begin(h)
    for h in range(2):
        local[h] = gram_term(half_rows(prior, h))
    for h in range(2):
        reduce_onward(h)
    for h in range(2):
        start = reduce_end(h) - local[h]
        residual[h] = start
        direction[h] = start
        norms.append(row_sum(start, start))
        lower(h, start)
        gather_begin(h)
    for h in range(2):
        gather_onward(h)
        local[h] = gram_term(direction[h])

    def iterate(step, norms):
        for h in range(2):
            gather_end(h)
            accumulate(h, False)
            reduce_begin(h)
        for h in range(2):
            reduce_onward(h)
        fresh = []
        for h in range(2):
            image = local[h] + reduce_end(h)
            d = direction[h]
            alpha = norms[h] / (row_sum(d, image) + EPS)
            for t in range(2):
                rows = slice(t * tile + h * half, t * tile + (h + 1) * half)
                block = slice(t * half, (t + 1) * half)
                out[rows] = out[rows] + alpha[block] * d[block]
            r = residual[h] - alpha * image
            residual[h] = r
            fresh.append(row_sum(r, r))
            after = r + fresh[h] / (norms[h] + EPS) * d
            direction[h] = after

            @pl.when(step < ITERS - 1)
            def _():
                lower(h, after)
                gather_begin(h)

        @pl.when(step < ITERS - 1)
        def _():
            for h in range(2):
                gather_onward(h)
                local[h] = gram_term(direction[h])

        return tuple(fresh)

    lax.fori_loop(0, ITERS, iterate, tuple(norms))


def body(user_prior, item_factors, user_tiles, item_tiles, counts):
    n_blk = lax.axis_size("blk")
    n_grp = lax.axis_size("grp")
    n_all = n_blk * n_grp
    pairs, tile, _ = counts.shape
    rank = item_factors.shape[1]
    users = 2 * n_grp
    own = user_prior.shape[0]
    held = item_factors.shape[0] // tile
    half = tile // 2
    grows = rank // n_grp
    vmem = pl.BlockSpec(memory_space=pltpu.VMEM)
    smem = pl.BlockSpec(memory_space=pltpu.SMEM)
    dma = pltpu.SemaphoreType.DMA
    low_type, whole_type, full = jnp.bfloat16, jnp.int16, jnp.float32
    return pl.pallas_call(
        functools.partial(kernel, n_blk, n_grp),
        out_shape=jax.ShapeDtypeStruct((own, rank), full),
        in_specs=[smem, smem, vmem, vmem, pl.BlockSpec(memory_space=pl.ANY)],
        out_specs=vmem,
        scratch_shapes=[
            pltpu.VMEM((1, 128), jnp.int32),
            pltpu.VMEM((n_all, 1, 128), jnp.int32),
            pltpu.SMEM((n_all, 1, 128), jnp.int32),
            pltpu.VMEM((8, 128), jnp.int32),
            pltpu.SMEM((8, 128), jnp.int32),
            *(pltpu.VMEM((CLOSE, held, rows, rank), low_type) for _, rows in SHARE),
            *(pltpu.VMEM((held, rows, rank), low_type) for _, rows in SHARE),
            *(pltpu.VMEM((FACE, SIDE, 2, rows, rank), low_type) for _, rows in SHARE),
            *(pltpu.VMEM((FACE, SIDE, 2, rows, rank), low_type) for _, rows in SHARE),
            pltpu.VMEM((pairs, tile, rank), low_type),
            pltpu.VMEM((pairs, tile, tile), jnp.int32),
            pltpu.VMEM((pairs, tile, tile), low_type),
            pltpu.VMEM((pairs, tile, tile), low_type),
            pltpu.VMEM((pairs, half, tile), low_type),
            pltpu.VMEM((users, half, rank), low_type),
            pltpu.VMEM((users, half, rank), low_type),
            pltpu.VMEM((2, pairs + 1, half, rank), full),
            pltpu.VMEM((n_grp, grows, rank), full),
            pltpu.VMEM((n_grp, grows, rank), full),
            pltpu.VMEM((n_blk, grows, rank), full),
            pltpu.VMEM((n_grp, grows, rank), full),
            pltpu.VMEM((2, grows, rank), full),
            pltpu.VMEM((2, 2, SIDE, SIDE, half, rank), whole_type),
            pltpu.VMEM((2, 2, SIDE, SIDE, 1, rank), full),
            pltpu.VMEM((2, 2, SIDE, SIDE, half, rank), whole_type),
            pltpu.VMEM((2, 2, SIDE, SIDE, 1, rank), full),
            pltpu.VMEM((2, 2, SIDE, half, rank), whole_type),
            pltpu.VMEM((2, 2, SIDE, 1, rank), full),
            pltpu.VMEM((2, 2, SIDE, half, rank), whole_type),
            pltpu.VMEM((2, 2, SIDE, 1, rank), full),
            pltpu.VMEM((2, 2, half, rank), full),
            pltpu.VMEM((2, tile, rank), full),
            pltpu.VMEM((2, tile, rank), full),
            pltpu.VMEM((2, tile, rank), full),
            dma((2, PEERS + 1)),
            dma((2, 3, 4)),
            dma((2, 2, 3, FACE)),
            dma((2, 2, 2, SIDE)),
            dma((2, 2, 2, SIDE, SIDE)),
            dma((2, 2, 2, 2, SIDE, SIDE)),
            dma((2, 2, 2, 2, SIDE)),
            dma((3, 2, n_grp)),
            dma((3,)),
        ],
        compiler_params=pltpu.CompilerParams(
            collective_id=0, has_side_effects=True, vmem_limit_bytes=60 << 20
        ),
        name="als",
    )(item_tiles, user_tiles, item_factors.reshape(held, tile, rank), user_prior, counts)


def solution(mesh):
    in_specs = (
        P(("blk", "grp"), None),
        P(("blk", "grp"), None),
        P(("blk", "grp")),
        P(("blk", "grp")),
        P(("blk", "grp"), None, None),
    )
    out_specs = P(("blk", "grp"), None)
    return jax.shard_map(body, mesh=mesh, in_specs=in_specs, out_specs=out_specs, check_vma=False)
```

```python
import functools

import jax
import jax.numpy as jnp
from jax import lax
from jax.experimental import pallas as pl
from jax.experimental.pallas import tpu as pltpu
from jax.sharding import PartitionSpec as P

ITERS = 3
ALPHA = 40.0
REG = 32.0
EPS = 1e-06
SIDE = 4
PLANE = SIDE * SIDE
FACE = 2 * PLANE
PEERS = 73
LEVELS = 32700.0
SHARE = ((0, 48), (48, 48), (96, 32))
AROUND = (0, 1, 3, 2)
CLOSE = 3
SHIFTS = (1, 3, 4, 12, 2, 8, 5, 15, 7, 13, 6, 14, 9, 11, 10)
MESH = pl.DeviceIdType.MESH


def position():
    b = lax.axis_index("blk")
    g = lax.axis_index("grp")
    return (g // SIDE, g % SIDE, b // 2), b % 2


def mesh_id(place, core):
    x, y, z = place
    return z * 2 + core, x * SIDE + y


def flat_id(place, core):
    b, g = mesh_id(place, core)
    return b * PLANE + g


def moved(place, axis, k):
    return tuple((v + k) % SIDE if i == axis else v for i, v in enumerate(place))


def put_at(place, axis, value):
    return tuple(value if i == axis else v for i, v in enumerate(place))


def remote(src, dst, send_sem, recv_sem, device):
    return pltpu.make_async_remote_copy(
        src_ref=src, dst_ref=dst, send_sem=send_sem, recv_sem=recv_sem,
        device_id=device, device_id_type=MESH,
    )


def quantize(value):
    top = jnp.maximum(jnp.max(jnp.abs(value), axis=0, keepdims=True), 1e-30)
    whole = jnp.round(value * (LEVELS / top)).astype(jnp.int32).astype(jnp.int16)
    return whole, top * (1.0 / LEVELS)


def restore(whole, unit):
    return whole.astype(jnp.int32).astype(jnp.float32) * unit


def tile_place(u):
    g = u // 2
    x, y = g // SIDE, g % SIDE
    return jnp.where(u % 2 == 0, y * SIDE + x, PLANE + x * SIDE + y)


def kernel(
    n_blk, n_grp,
    wanted_tiles, user_tiles, items, prior, counts,
    out,
    req, reqs, want, table, table_s,
    ring0, ring1, ring2, far0, far1, far2, send0, send1, send2, recv0, recv1, recv2,
    tiles, counted, weights, pulls, scaled, low0, low1, chain,
    gram_own, gram_a, gram_b, gram_c, gram_t,
    part_q, part_u, first_q, first_u, sum_q, sum_u, second_q, second_u, sums,
    residual, direction, local,
    req_sems, ring_sems, tile_sems, gather_one, gather_two, first_sems, second_sems,
    gram_sems, local_sems,
):
    n_all = n_blk * n_grp
    place, core = position()
    x, y, z = place
    b, g = mesh_id(place, core)
    me = b * n_grp + g
    pairs, tile, rank = tiles.shape
    held = items.shape[0]
    half = tile // 2
    fars = (far0, far1, far2)
    lows = (low0, low1)
    rings, sends, recvs = (ring0, ring1, ring2), (send0, send1, send2), (recv0, recv1, recv2)

    def half_rows(ref, h):
        return jnp.concatenate(
            [ref[t * tile + h * half:t * tile + (h + 1) * half] for t in range(2)], axis=0
        )

    def lower(h, vectors):
        d_low = vectors.astype(jnp.bfloat16)
        lows[h][y * SIDE + x] = d_low[:half]
        lows[h][PLANE + x * SIDE + y] = d_low[half:]

    count_copy = pltpu.make_async_copy(counts, counted, local_sems.at[0])
    count_copy.start()

    def same_x(i):
        return (place[0], (y + i // 8) % SIDE, (z + i // 2) % SIDE), (core + i) % 2

    def same_y(i):
        return ((x + 1 + i // 8) % SIDE, place[1], (z + i // 2) % SIDE), (core + i) % 2

    def same_z(i):
        return ((x + 1 + i // 2 % 3) % SIDE, (y + 1 + i // 6) % SIDE, place[2]), (core + i) % 2

    families = ((same_x, 1, 32, 0), (same_y, 0, 24, 32), (same_z, 0, 18, 56))

    def for_peers(act):
        for family, first, last, base in families:
            def one(i, carry):
                act(mesh_id(*family(i)), base + i)
                return carry

            lax.fori_loop(first, last, one, 0)

    barrier = pltpu.get_barrier_semaphore()
    for_peers(
        lambda to, i: pl.semaphore_signal(barrier, inc=1, device_id=to, device_id_type=MESH)
    )

    lane = lax.broadcasted_iota(jnp.int32, (1, 128), 1)
    zero = jnp.zeros((1, 128), jnp.int32)

    def ask(i, state):
        first, second = state
        for j in range(8):
            p = i * 8 + j
            late, early = wanted_tiles[p], wanted_tiles[pairs - 1 - p]
            second = jnp.where(lane == late // held, late % held, second)
            first = jnp.where(lane == early // held, early % held, first)
        return first, second

    first, second = lax.fori_loop(0, pairs // 8, ask, (zero, zero))
    asked = first + 256 * second
    req[...] = asked
    reqs[me] = asked
    for h in range(2):
        lower(h, half_rows(prior, h))

    def keep(i, carry):
        for axis, (start, rows) in enumerate(SHARE):
            rings[axis][0, i] = items[i, start:start + rows]
        return carry

    lax.fori_loop(0, held, keep, 0)

    pl.semaphore_wait(barrier, PEERS)

    def request(to, i):
        return remote(req, reqs.at[me], req_sems.at[0, i], req_sems.at[1, i], to)

    for_peers(lambda to, i: request(to, i).start())

    def ring_copy(axis, kind):
        start, rows = SHARE[axis]
        source = 2 if kind % 2 == 0 else 1
        if kind < 2:
            src, dst = items.at[:, pl.ds(start, rows)], rings[axis].at[source]
        else:
            half = pl.ds(0 if kind == 2 else held // 2, held // 2)
            src, dst = rings[axis].at[source, half], fars[axis].at[half]
        to = moved(place, axis, 1 if kind % 2 == 0 else SIDE - 1)
        return remote(
            src, dst, ring_sems.at[0, axis, kind], ring_sems.at[1, axis, kind],
            mesh_id(to, core),
        )

    for kind in range(2):
        for axis in range(3):
            ring_copy(axis, kind).start()

    def low_place(t, m):
        if t == 0:
            return y * SIDE + (x + SIDE - m) % SIDE
        return PLANE + x * SIDE + (y + SIDE - m) % SIDE

    def gather_a(h, t, k):
        ref = lows[h].at[low_place(t, 0)]
        return remote(
            ref, ref, gather_one.at[0, h, t, k], gather_one.at[1, h, t, k],
            mesh_id(moved(place, t, k), core),
        )

    def gather_b(h, t, k, m):
        ref = lows[h].at[low_place(t, m)]
        return remote(
            ref, ref, gather_two.at[0, h, t, k, m], gather_two.at[1, h, t, k, m],
            mesh_id(moved(place, 1 - t, k), core),
        )

    def gather_begin(h):
        for k in range(1, SIDE):
            for t in range(2):
                gather_a(h, t, k).start()
        for k in range(1, SIDE):
            for t in range(2):
                gather_b(h, t, k, 0).start()

    def gather_onward(h):
        for m in range(1, SIDE):
            for t in range(2):
                gather_a(h, t, m).wait()
                for k in range(1, SIDE):
                    gather_b(h, t, k, m).start()

    def gather_end(h):
        for m in range(SIDE):
            for k in range(1, SIDE):
                for t in range(2):
                    gather_b(h, t, k, m).wait()

    gather_begin(0)
    gather_begin(1)

    chunk = min(8, held)

    def gram_step(i, total):
        block = items[pl.ds(i * chunk, chunk)].reshape(chunk * tile, rank)
        return total + lax.dot_general(
            block, block, (((0,), (0,)), ((), ())), preferred_element_type=jnp.float32
        )

    gram_own[...] = lax.fori_loop(
        0, held // chunk, gram_step, jnp.zeros((rank, rank), jnp.float32)
    ).reshape(n_grp, rank // n_grp, rank)

    def gram_first(k):
        to = (g + k) % n_grp
        return remote(
            gram_own.at[to], gram_a.at[k], gram_sems.at[0, 0, k], gram_sems.at[0, 1, k], (b, to)
        )

    def gram_second(k):
        return remote(
            gram_t.at[0], gram_b.at[k], gram_sems.at[1, 0, k], gram_sems.at[1, 1, k],
            ((b + k) % n_blk, g),
        )

    def gram_third(k):
        return remote(
            gram_t.at[1], gram_c.at[g], gram_sems.at[2, 0, k], gram_sems.at[2, 1, k],
            (b, (g + k) % n_grp),
        )

    for k in range(1, n_grp):
        gram_first(k).start()

    for_peers(lambda to, i: request(to, i).wait())
    want_copy = pltpu.make_async_copy(reqs, want, local_sems.at[1])
    want_copy.start()
    for axis in range(3):
        for kind in range(2):
            ring_copy(axis, kind).wait()
            ring_copy(axis, kind + 2).start()
    want_copy.wait()

    def face_shift(turn):
        words = [sum(v << 4 * j for j, v in enumerate(SHIFTS[i:i + 7])) for i in (0, 7, 14)]
        last = turn >= 28
        i = jnp.where(last, 14, turn // 4 * 2 + turn % 2)
        flip = jnp.where(last, turn % 2, turn // 2 % 2)
        word = jnp.where(i < 7, words[0], jnp.where(i < 14, words[1], words[2]))
        shift = lax.shift_right_logical(jnp.int32(word), 4 * (i % 7)) % 16
        return shift * 2 + flip

    def face_target(axis, step):
        a, c = step // 2 // SIDE, step // 2 % SIDE
        a = jnp.where(core == 0, a, (SIDE - a) % SIDE)
        c = jnp.where(core == 0, c, (SIDE - c) % SIDE)
        to = moved(moved(place, (axis + 1) % 3, a), (axis + 2) % 3, c)
        return to, (core + step) % 2

    def face_index(axis):
        return (place[(axis + 1) % 3] * SIDE + place[(axis + 2) % 3]) * 2 + core

    def pack_into(ref, slot, axis, to, which):
        for i in which:
            w = (place[axis] + AROUND[i]) % SIDE
            pair = want[to, 0, flat_id(put_at(place, axis, w), core)]
            for j, held_at in enumerate((pair % 256, pair // 256)):
                ref[slot, i, j] = rings[axis][i, held_at] if i < CLOSE else fars[axis][held_at]

    levels = (tuple(range(CLOSE)), tuple(range(CLOSE, SIDE)))

    def pack(level, step):
        for axis in range(3):
            to, to_core = face_target(axis, step)
            pack_into(sends[axis], step, axis, flat_id(to, to_core), levels[level])

    def parcel(level, axis, step):
        to, to_core = face_target(axis, step)
        part = pl.ds(levels[level][0], len(levels[level]))
        return remote(
            sends[axis].at[step, part], recvs[axis].at[face_index(axis), part],
            tile_sems.at[0, level, axis, step], tile_sems.at[1, level, axis, step],
            mesh_id(to, to_core),
        )

    def ship(level, first, last):
        pack(level, face_shift(first))

        def one(turn, carry):
            pack(level, face_shift(turn + 1))
            for axis in range(3):
                parcel(level, axis, face_shift(turn)).start()
            return carry

        lax.fori_loop(first, last - 1, one, 0)
        for axis in range(3):
            parcel(level, axis, face_shift(last - 1)).start()

    turns_all = 2 * len(SHIFTS)
    ship(0, 0, 4)
    gather_onward(0)
    gather_onward(1)
    for k in range(1, n_grp):
        gram_first(k).wait()
    part = gram_own[g]
    for k in range(1, n_grp):
        part = part + gram_a[k]
    gram_t[0] = part
    ship(0, 4, 16)
    for k in range(1, n_blk):
        gram_second(k).start()
    ship(0, 16, turns_all)
    for k in range(1, n_blk):
        gram_second(k).wait()
    part = gram_t[0]
    for k in range(1, n_blk):
        part = part + gram_b[k]
    gram_t[1] = part
    gram_c[g] = part
    for axis in range(3):
        for kind in range(2, 4):
            ring_copy(axis, kind).wait()
    pack(0, 1)
    pack(1, 1)
    ship(1, 0, turns_all)
    for level in range(2):
        for axis in range(3):
            parcel(level, axis, 1).start()
    for k in range(1, n_grp):
        gram_third(k).start()
    for axis in range(3):
        pack_into(recvs[axis], face_index(axis), axis, me, range(SIDE))

    def link(p, state):
        seen, order, last, before = state
        owner = wanted_tiles[p] // held
        hit = lane == owner
        turn = jnp.sum(jnp.where(hit, seen, 0), axis=1, keepdims=True)
        order = jnp.where(lane == p, owner * 2 + jnp.minimum(turn, 1), order)
        seen = jnp.where(hit, 1, seen)
        mine = lane == user_tiles[p]
        earlier = jnp.sum(jnp.where(mine, last, 0), axis=1, keepdims=True)
        before = jnp.where(lane == p, earlier, before)
        last = jnp.where(mine, p + 1, last)
        return seen, order, last, before

    _, order, last, before = lax.fori_loop(0, pairs, link, (zero,) * 4)
    row = lax.broadcasted_iota(jnp.int32, (8, 128), 0)
    table[...] = jnp.where(
        row == 0, order, jnp.where(row == 1, before, jnp.where(row == 2, last, 0))
    )
    table_copy = pltpu.make_async_copy(table, table_s, local_sems.at[2])
    table_copy.start()
    count_copy.wait()

    def weigh(p, carry):
        weight = counted[p].astype(jnp.float32) * ALPHA
        weights[p] = weight.astype(jnp.bfloat16)
        pulls[p] = jnp.where(weight > 0, 1.0 + weight, 0.0).astype(jnp.bfloat16)
        return carry

    lax.fori_loop(0, pairs, weigh, 0)
    for h in range(2):
        chain[h, 0] = jnp.zeros((half, rank), jnp.float32)
    table_copy.wait()

    gather_end(0)
    gather_end(1)
    for k in range(1, n_grp):
        gram_third(k).wait()

    def wait_parcel(step, carry):
        for level in range(2):
            for axis in range(3):
                parcel(level, axis, step).wait()
        return carry

    lax.fori_loop(1, FACE, wait_parcel, 0)

    def take(i, carry):
        for j in range(4):
            p = i * 4 + j
            slot = table_s[0, p]
            owner, turn = slot // 2, slot % 2
            ob, og = owner // n_grp, owner % n_grp
            at, of = (og // SIDE, og % SIDE, ob // 2), ob % 2
            for axis, (start, rows) in enumerate(SHARE):
                face = (at[(axis + 1) % 3] * SIDE + at[(axis + 2) % 3]) * 2 + of
                ahead = (at[axis] + SIDE - place[axis]) % SIDE
                ahead = jnp.where(ahead >= 2, 5 - ahead, ahead)
                tiles[p, start:start + rows] = recvs[axis][face, ahead, turn]
        return carry

    lax.fori_loop(0, pairs // 4, take, 0)

    group = 8

    def score_all(h):
        part = slice(h * half, (h + 1) * half)

        def score(i, carry):
            for j in range(group):
                p = i * group + j
                scores = lax.dot_general(
                    lows[h][tile_place(user_tiles[p])], tiles[p], (((1,), (1,)), ((), ())),
                    preferred_element_type=jnp.float32,
                )
                scaled[p] = (weights[p, part].astype(jnp.float32) * scores).astype(jnp.bfloat16)
            return carry

        lax.fori_loop(0, pairs // group, score, 0)

    def spread_all(h, with_rhs):
        part = slice(h * half, (h + 1) * half)

        def spread(i, carry):
            backs = []
            for j in range(group):
                p = i * group + j
                back = jnp.dot(scaled[p], tiles[p], preferred_element_type=jnp.float32)
                if with_rhs:
                    pulled = jnp.dot(
                        pulls[p, part], tiles[p], preferred_element_type=jnp.float32
                    )
                    back = pulled - back
                backs.append(back)
            for j in range(group):
                p = i * group + j
                chain[h, p + 1] = chain[h, table_s[1, p]] + backs[j]
            return carry

        lax.fori_loop(0, pairs // group, spread, 0)

    near, far = (y, x), (x, y)

    def partial(h, t, away, end):
        u = 2 * (end * SIDE + away) if t == 0 else 2 * (away * SIDE + end) + 1
        return chain[h, table_s[2, u]]

    def sum_first(h, t, k, m):
        to = mesh_id(moved(place, 1 - t, k), core)
        return [
            remote(
                src.at[h, t, k, m], dst.at[h, t, k, m], first_sems.at[0, i, h, t, k, m],
                first_sems.at[1, i, h, t, k, m], to,
            )
            for i, (src, dst) in enumerate(((part_u, first_u), (part_q, first_q)))
        ]

    def sum_second(h, t, m):
        to = mesh_id(moved(place, t, m), core)
        return [
            remote(
                src.at[h, t, m], dst.at[h, t, m], second_sems.at[0, i, h, t, m],
                second_sems.at[1, i, h, t, m], to,
            )
            for i, (src, dst) in enumerate(((sum_u, second_u), (sum_q, second_q)))
        ]

    turns = tuple(range(1, SIDE)) + (0,)

    def reduce_begin(h):
        for m in turns:
            for k in range(1, SIDE):
                for t in range(2):
                    whole, unit = quantize(
                        partial(h, t, (near[t] + k) % SIDE, (far[t] + m) % SIDE)
                    )
                    part_q[h, t, k, m] = whole
                    part_u[h, t, k, m] = unit
                    for copy in sum_first(h, t, k, m):
                        copy.start()

    def reduce_onward(h):
        for m in turns:
            for t in range(2):
                total = partial(h, t, near[t], (far[t] + m) % SIDE)
                for k in range(1, SIDE):
                    for copy in sum_first(h, t, k, m):
                        copy.wait()
                    total = total + restore(first_q[h, t, k, m], first_u[h, t, k, m])
                if m == 0:
                    sums[h, t] = total
                else:
                    whole, unit = quantize(total)
                    sum_q[h, t, m] = whole
                    sum_u[h, t, m] = unit
                    for copy in sum_second(h, t, m):
                        copy.start()

    def reduce_end(h):
        totals = []
        for t in range(2):
            total = sums[h, t]
            for m in range(1, SIDE):
                for copy in sum_second(h, t, m):
                    copy.wait()
                total = total + restore(second_q[h, t, m], second_u[h, t, m])
            totals.append(total)
        return jnp.concatenate(totals, axis=0)

    def gram_term(vectors):
        return (
            jnp.dot(vectors, gram_c[...].reshape(rank, rank), precision=lax.Precision.HIGHEST,
                    preferred_element_type=jnp.float32)
            + REG * vectors
        )

    def row_sum(left, right):
        return jnp.sum(left * right, axis=1, keepdims=True)

    def products(with_rhs):
        score_all(0)
        if not with_rhs:
            gather_onward(1)
        spread_all(0, with_rhs)
        reduce_begin(0)
        if not with_rhs:
            gather_end(1)
        score_all(1)
        reduce_onward(0)
        spread_all(1, with_rhs)
        reduce_begin(1)

    def launch(h, vectors):
        lower(h, vectors)
        gather_begin(h)
        local[h] = gram_term(vectors)

    norms = []
    out[...] = prior[...]
    for h in range(2):
        local[h] = gram_term(half_rows(prior, h))
    products(True)
    for h in range(2):
        if h == 1:
            reduce_onward(1)
            gather_onward(0)
        start = reduce_end(h) - local[h]
        residual[h] = start
        direction[h] = start
        norms.append(row_sum(start, start))
        launch(h, start)

    def iterate(step, norms):
        more = step < ITERS - 1
        gather_end(0)
        products(False)
        fresh = []
        for h in range(2):
            if h == 1:
                reduce_onward(1)
                pl.when(more)(functools.partial(gather_onward, 0))
            image = local[h] + reduce_end(h)
            d = direction[h]
            alpha = norms[h] / (row_sum(d, image) + EPS)
            for t in range(2):
                rows = slice(t * tile + h * half, t * tile + (h + 1) * half)
                block = slice(t * half, (t + 1) * half)
                out[rows] = out[rows] + alpha[block] * d[block]
            r = residual[h] - alpha * image
            residual[h] = r
            fresh.append(row_sum(r, r))
            after = r + fresh[h] / (norms[h] + EPS) * d
            direction[h] = after
            pl.when(more)(functools.partial(launch, h, after))

        return tuple(fresh)

    lax.fori_loop(0, ITERS, iterate, tuple(norms))


def body(user_prior, item_factors, user_tiles, item_tiles, counts):
    n_blk = lax.axis_size("blk")
    n_grp = lax.axis_size("grp")
    n_all = n_blk * n_grp
    pairs, tile, _ = counts.shape
    rank = item_factors.shape[1]
    users = 2 * n_grp
    own = user_prior.shape[0]
    held = item_factors.shape[0] // tile
    half = tile // 2
    grows = rank // n_grp
    vmem = pl.BlockSpec(memory_space=pltpu.VMEM)
    smem = pl.BlockSpec(memory_space=pltpu.SMEM)
    dma = pltpu.SemaphoreType.DMA
    low_type, whole_type, full = jnp.bfloat16, jnp.int16, jnp.float32
    return pl.pallas_call(
        functools.partial(kernel, n_blk, n_grp),
        out_shape=jax.ShapeDtypeStruct((own, rank), full),
        in_specs=[smem, smem, vmem, vmem, pl.BlockSpec(memory_space=pl.ANY)],
        out_specs=vmem,
        scratch_shapes=[
            pltpu.VMEM((1, 128), jnp.int32),
            pltpu.VMEM((n_all, 1, 128), jnp.int32),
            pltpu.SMEM((n_all, 1, 128), jnp.int32),
            pltpu.VMEM((8, 128), jnp.int32),
            pltpu.SMEM((8, 128), jnp.int32),
            *(pltpu.VMEM((CLOSE, held, rows, rank), low_type) for _, rows in SHARE),
            *(pltpu.VMEM((held, rows, rank), low_type) for _, rows in SHARE),
            *(pltpu.VMEM((FACE, SIDE, 2, rows, rank), low_type) for _, rows in SHARE),
            *(pltpu.VMEM((FACE, SIDE, 2, rows, rank), low_type) for _, rows in SHARE),
            pltpu.VMEM((pairs, tile, rank), low_type),
            pltpu.VMEM((pairs, tile, tile), jnp.int32),
            pltpu.VMEM((pairs, tile, tile), low_type),
            pltpu.VMEM((pairs, tile, tile), low_type),
            pltpu.VMEM((pairs, half, tile), low_type),
            pltpu.VMEM((users, half, rank), low_type),
            pltpu.VMEM((users, half, rank), low_type),
            pltpu.VMEM((2, pairs + 1, half, rank), full),
            pltpu.VMEM((n_grp, grows, rank), full),
            pltpu.VMEM((n_grp, grows, rank), full),
            pltpu.VMEM((n_blk, grows, rank), full),
            pltpu.VMEM((n_grp, grows, rank), full),
            pltpu.VMEM((2, grows, rank), full),
            pltpu.VMEM((2, 2, SIDE, SIDE, half, rank), whole_type),
            pltpu.VMEM((2, 2, SIDE, SIDE, 1, rank), full),
            pltpu.VMEM((2, 2, SIDE, SIDE, half, rank), whole_type),
            pltpu.VMEM((2, 2, SIDE, SIDE, 1, rank), full),
            pltpu.VMEM((2, 2, SIDE, half, rank), whole_type),
            pltpu.VMEM((2, 2, SIDE, 1, rank), full),
            pltpu.VMEM((2, 2, SIDE, half, rank), whole_type),
            pltpu.VMEM((2, 2, SIDE, 1, rank), full),
            pltpu.VMEM((2, 2, half, rank), full),
            pltpu.VMEM((2, tile, rank), full),
            pltpu.VMEM((2, tile, rank), full),
            pltpu.VMEM((2, tile, rank), full),
            dma((2, PEERS + 1)),
            dma((2, 3, 4)),
            dma((2, 2, 3, FACE)),
            dma((2, 2, 2, SIDE)),
            dma((2, 2, 2, SIDE, SIDE)),
            dma((2, 2, 2, 2, SIDE, SIDE)),
            dma((2, 2, 2, 2, SIDE)),
            dma((3, 2, n_grp)),
            dma((3,)),
        ],
        compiler_params=pltpu.CompilerParams(
            collective_id=0, has_side_effects=True, vmem_limit_bytes=60 << 20
        ),
        name="als",
    )(item_tiles, user_tiles, item_factors.reshape(held, tile, rank), user_prior, counts)


def solution(mesh):
    in_specs = (
        P(("blk", "grp"), None),
        P(("blk", "grp"), None),
        P(("blk", "grp")),
        P(("blk", "grp")),
        P(("blk", "grp"), None, None),
    )
    out_specs = P(("blk", "grp"), None)
    return jax.shard_map(body, mesh=mesh, in_specs=in_specs, out_specs=out_specs, check_vma=False)
```

```python
import functools

import jax
import jax.numpy as jnp
from jax import lax
from jax.experimental import pallas as pl
from jax.experimental.pallas import tpu as pltpu
from jax.sharding import PartitionSpec as P

ITERS = 3
ALPHA = 40.0
REG = 32.0
EPS = 1e-06
SIDE = 4
PLANE = SIDE * SIDE
FACE = 2 * PLANE
PEERS = 73
LEVELS = 32700.0
SHARE = ((0, 48), (48, 48), (96, 32))
AROUND = (0, 1, 3, 2)
CLOSE = 3
SHIFTS = (1, 3, 4, 12, 2, 8, 5, 15, 7, 13, 6, 14, 9, 11, 10)
MESH = pl.DeviceIdType.MESH


def position():
    b = lax.axis_index("blk")
    g = lax.axis_index("grp")
    return (g // SIDE, g % SIDE, b // 2), b % 2


def mesh_id(place, core):
    x, y, z = place
    return z * 2 + core, x * SIDE + y


def flat_id(place, core):
    b, g = mesh_id(place, core)
    return b * PLANE + g


def moved(place, axis, k):
    return tuple((v + k) % SIDE if i == axis else v for i, v in enumerate(place))


def put_at(place, axis, value):
    return tuple(value if i == axis else v for i, v in enumerate(place))


def remote(src, dst, send_sem, recv_sem, device):
    return pltpu.make_async_remote_copy(
        src_ref=src, dst_ref=dst, send_sem=send_sem, recv_sem=recv_sem,
        device_id=device, device_id_type=MESH,
    )


def quantize(value):
    top = jnp.maximum(jnp.max(jnp.abs(value), axis=0, keepdims=True), 1e-30)
    whole = jnp.round(value * (LEVELS / top)).astype(jnp.int32).astype(jnp.int16)
    return whole, top * (1.0 / LEVELS)


def restore(whole, unit):
    return whole.astype(jnp.int32).astype(jnp.float32) * unit


def tile_place(u):
    g = u // 2
    x, y = g // SIDE, g % SIDE
    return jnp.where(u % 2 == 0, y * SIDE + x, PLANE + x * SIDE + y)


def kernel(
    n_blk, n_grp,
    wanted_tiles, user_tiles, items, prior, counts,
    out,
    req, reqs, want, table, table_s,
    ring0, ring1, ring2, far0, far1, far2, send0, send1, send2, recv0, recv1, recv2,
    tiles, counted, weights, pulls, scaled, low0, low1, chain,
    gram_own, gram_a, gram_b, gram_c, gram_t,
    part_q, part_u, first_q, first_u, sum_q, sum_u, second_q, second_u, sums,
    residual, direction, local,
    req_sems, ring_sems, tile_sems, gather_one, gather_two, first_sems, second_sems,
    gram_sems, local_sems,
):
    n_all = n_blk * n_grp
    place, core = position()
    x, y, z = place
    b, g = mesh_id(place, core)
    me = b * n_grp + g
    pairs, tile, rank = tiles.shape
    held = items.shape[0]
    half = tile // 2
    fars = (far0, far1, far2)
    lows = (low0, low1)
    rings, sends, recvs = (ring0, ring1, ring2), (send0, send1, send2), (recv0, recv1, recv2)

    def half_rows(ref, h):
        return jnp.concatenate(
            [ref[t * tile + h * half:t * tile + (h + 1) * half] for t in range(2)], axis=0
        )

    def lower(h, vectors):
        d_low = vectors.astype(jnp.bfloat16)
        lows[h][y * SIDE + x] = d_low[:half]
        lows[h][PLANE + x * SIDE + y] = d_low[half:]

    count_copy = pltpu.make_async_copy(counts, counted, local_sems.at[0])
    count_copy.start()

    def same_x(i):
        return (place[0], (y + i // 8) % SIDE, (z + i // 2) % SIDE), (core + i) % 2

    def same_y(i):
        return ((x + 1 + i // 8) % SIDE, place[1], (z + i // 2) % SIDE), (core + i) % 2

    def same_z(i):
        return ((x + 1 + i // 2 % 3) % SIDE, (y + 1 + i // 6) % SIDE, place[2]), (core + i) % 2

    families = ((same_x, 1, 32, 0), (same_y, 0, 24, 32), (same_z, 0, 18, 56))

    def for_peers(act):
        for family, first, last, base in families:
            def one(i, carry):
                act(mesh_id(*family(i)), base + i)
                return carry

            lax.fori_loop(first, last, one, 0)

    barrier = pltpu.get_barrier_semaphore()
    for_peers(
        lambda to, i: pl.semaphore_signal(barrier, inc=1, device_id=to, device_id_type=MESH)
    )

    lane = lax.broadcasted_iota(jnp.int32, (1, 128), 1)
    zero = jnp.zeros((1, 128), jnp.int32)

    def ask(i, state):
        first, second = state
        for j in range(8):
            p = i * 8 + j
            late, early = wanted_tiles[p], wanted_tiles[pairs - 1 - p]
            second = jnp.where(lane == late // held, late % held, second)
            first = jnp.where(lane == early // held, early % held, first)
        return first, second

    first, second = lax.fori_loop(0, pairs // 8, ask, (zero, zero))
    asked = first + 256 * second
    req[...] = asked
    reqs[me] = asked
    for h in range(2):
        lower(h, half_rows(prior, h))

    def keep(i, carry):
        for axis, (start, rows) in enumerate(SHARE):
            rings[axis][0, i] = items[i, start:start + rows]
        return carry

    lax.fori_loop(0, held, keep, 0)

    pl.semaphore_wait(barrier, PEERS)

    def request(to, i):
        return remote(req, reqs.at[me], req_sems.at[0, i], req_sems.at[1, i], to)

    for_peers(lambda to, i: request(to, i).start())

    def ring_copy(axis, kind):
        start, rows = SHARE[axis]
        source = 2 if kind % 2 == 0 else 1
        if kind < 2:
            src, dst = items.at[:, pl.ds(start, rows)], rings[axis].at[source]
        else:
            half = pl.ds(0 if kind == 2 else held // 2, held // 2)
            src, dst = rings[axis].at[source, half], fars[axis].at[half]
        to = moved(place, axis, 1 if kind % 2 == 0 else SIDE - 1)
        return remote(
            src, dst, ring_sems.at[0, axis, kind], ring_sems.at[1, axis, kind],
            mesh_id(to, core),
        )

    for kind in range(2):
        for axis in range(3):
            ring_copy(axis, kind).start()

    def gather_a(h, t, k):
        ref = lows[h].at[y * SIDE + x if t == 0 else PLANE + x * SIDE + y]
        return remote(
            ref, ref, gather_one.at[0, h, t, k], gather_one.at[1, h, t, k],
            mesh_id(moved(place, t, k), core),
        )

    def gather_b(h, t, k):
        ref = lows[h].at[pl.ds(y * SIDE if t == 0 else PLANE + x * SIDE, SIDE)]
        return remote(
            ref, ref, gather_two.at[0, h, t, k], gather_two.at[1, h, t, k],
            mesh_id(moved(place, 1 - t, k), core),
        )

    every = [(k, t) for k in (1, 3, 2) for t in range(2)]

    def gather_begin(h):
        for k, t in every:
            gather_a(h, t, k).start()

    def gather_onward(h):
        for k, t in every:
            gather_a(h, t, k).wait()
        for k, t in every:
            gather_b(h, t, k).start()

    def gather_end(h):
        for k, t in every:
            gather_b(h, t, k).wait()

    gather_begin(0)
    gather_begin(1)

    chunk = min(8, held)

    def gram_step(i, total):
        block = items[pl.ds(i * chunk, chunk)].reshape(chunk * tile, rank)
        return total + lax.dot_general(
            block, block, (((0,), (0,)), ((), ())), preferred_element_type=jnp.float32
        )

    gram_own[...] = lax.fori_loop(
        0, held // chunk, gram_step, jnp.zeros((rank, rank), jnp.float32)
    ).reshape(n_grp, rank // n_grp, rank)

    def gram_first(k):
        to = (g + k) % n_grp
        return remote(
            gram_own.at[to], gram_a.at[k], gram_sems.at[0, 0, k], gram_sems.at[0, 1, k], (b, to)
        )

    def gram_second(k):
        return remote(
            gram_t.at[0], gram_b.at[k], gram_sems.at[1, 0, k], gram_sems.at[1, 1, k],
            ((b + k) % n_blk, g),
        )

    def gram_third(k):
        return remote(
            gram_t.at[1], gram_c.at[g], gram_sems.at[2, 0, k], gram_sems.at[2, 1, k],
            (b, (g + k) % n_grp),
        )

    for k in range(1, n_grp):
        gram_first(k).start()

    for_peers(lambda to, i: request(to, i).wait())
    want_copy = pltpu.make_async_copy(reqs, want, local_sems.at[1])
    want_copy.start()
    for axis in range(3):
        for kind in range(2):
            ring_copy(axis, kind).wait()
            ring_copy(axis, kind + 2).start()
    want_copy.wait()

    def face_shift(turn):
        words = [sum(v << 4 * j for j, v in enumerate(SHIFTS[i:i + 7])) for i in (0, 7, 14)]
        last = turn >= 28
        i = jnp.where(last, 14, turn // 4 * 2 + turn % 2)
        flip = jnp.where(last, turn % 2, turn // 2 % 2)
        word = jnp.where(i < 7, words[0], jnp.where(i < 14, words[1], words[2]))
        shift = lax.shift_right_logical(jnp.int32(word), 4 * (i % 7)) % 16
        return shift * 2 + flip

    def face_target(axis, step):
        a, c = step // 2 // SIDE, step // 2 % SIDE
        a = jnp.where(core == 0, a, (SIDE - a) % SIDE)
        c = jnp.where(core == 0, c, (SIDE - c) % SIDE)
        to = moved(moved(place, (axis + 1) % 3, a), (axis + 2) % 3, c)
        return to, (core + step) % 2

    def face_index(axis):
        return (place[(axis + 1) % 3] * SIDE + place[(axis + 2) % 3]) * 2 + core

    def pack_into(ref, slot, axis, to, which):
        for i in which:
            w = (place[axis] + AROUND[i]) % SIDE
            pair = want[to, 0, flat_id(put_at(place, axis, w), core)]
            for j, held_at in enumerate((pair % 256, pair // 256)):
                ref[slot, i, j] = rings[axis][i, held_at] if i < CLOSE else fars[axis][held_at]

    levels = (tuple(range(CLOSE)), tuple(range(CLOSE, SIDE)))

    def pack(level, step):
        for axis in range(3):
            to, to_core = face_target(axis, step)
            pack_into(sends[axis], step, axis, flat_id(to, to_core), levels[level])

    def parcel(level, axis, step):
        to, to_core = face_target(axis, step)
        part = pl.ds(levels[level][0], len(levels[level]))
        return remote(
            sends[axis].at[step, part], recvs[axis].at[face_index(axis), part],
            tile_sems.at[0, level, axis, step], tile_sems.at[1, level, axis, step],
            mesh_id(to, to_core),
        )

    def ship(level, first, last):
        pack(level, face_shift(first))

        def one(turn, carry):
            pack(level, face_shift(turn + 1))
            for axis in range(3):
                parcel(level, axis, face_shift(turn)).start()
            return carry

        lax.fori_loop(first, last - 1, one, 0)
        for axis in range(3):
            parcel(level, axis, face_shift(last - 1)).start()

    turns_all = 2 * len(SHIFTS)
    ship(0, 0, 4)
    gather_onward(0)
    gather_onward(1)
    for k in range(1, n_grp):
        gram_first(k).wait()
    part = gram_own[g]
    for k in range(1, n_grp):
        part = part + gram_a[k]
    gram_t[0] = part
    ship(0, 4, 16)
    for k in range(1, n_blk):
        gram_second(k).start()
    ship(0, 16, turns_all)
    for k in range(1, n_blk):
        gram_second(k).wait()
    part = gram_t[0]
    for k in range(1, n_blk):
        part = part + gram_b[k]
    gram_t[1] = part
    gram_c[g] = part
    for axis in range(3):
        for kind in range(2, 4):
            ring_copy(axis, kind).wait()
    pack(0, 1)
    pack(1, 1)
    ship(1, 0, turns_all)
    for level in range(2):
        for axis in range(3):
            parcel(level, axis, 1).start()
    for k in range(1, n_grp):
        gram_third(k).start()
    for axis in range(3):
        pack_into(recvs[axis], face_index(axis), axis, me, range(SIDE))

    def link(p, state):
        seen, order, last, before = state
        owner = wanted_tiles[p] // held
        hit = lane == owner
        turn = jnp.sum(jnp.where(hit, seen, 0), axis=1, keepdims=True)
        order = jnp.where(lane == p, owner * 2 + jnp.minimum(turn, 1), order)
        seen = jnp.where(hit, 1, seen)
        mine = lane == user_tiles[p]
        earlier = jnp.sum(jnp.where(mine, last, 0), axis=1, keepdims=True)
        before = jnp.where(lane == p, earlier, before)
        last = jnp.where(mine, p + 1, last)
        return seen, order, last, before

    _, order, last, before = lax.fori_loop(0, pairs, link, (zero,) * 4)
    row = lax.broadcasted_iota(jnp.int32, (8, 128), 0)
    table[...] = jnp.where(
        row == 0, order, jnp.where(row == 1, before, jnp.where(row == 2, last, 0))
    )
    table_copy = pltpu.make_async_copy(table, table_s, local_sems.at[2])
    table_copy.start()
    count_copy.wait()

    def weigh(p, carry):
        weight = counted[p].astype(jnp.float32) * ALPHA
        weights[p] = weight.astype(jnp.bfloat16)
        pulls[p] = jnp.where(weight > 0, 1.0 + weight, 0.0).astype(jnp.bfloat16)
        return carry

    lax.fori_loop(0, pairs, weigh, 0)
    for h in range(2):
        chain[h, 0] = jnp.zeros((half, rank), jnp.float32)
    table_copy.wait()

    gather_end(0)
    gather_end(1)
    for k in range(1, n_grp):
        gram_third(k).wait()

    def wait_parcel(step, carry):
        for level in range(2):
            for axis in range(3):
                parcel(level, axis, step).wait()
        return carry

    lax.fori_loop(1, FACE, wait_parcel, 0)

    def take(i, carry):
        for j in range(4):
            p = i * 4 + j
            slot = table_s[0, p]
            owner, turn = slot // 2, slot % 2
            ob, og = owner // n_grp, owner % n_grp
            at, of = (og // SIDE, og % SIDE, ob // 2), ob % 2
            for axis, (start, rows) in enumerate(SHARE):
                face = (at[(axis + 1) % 3] * SIDE + at[(axis + 2) % 3]) * 2 + of
                ahead = (at[axis] + SIDE - place[axis]) % SIDE
                ahead = jnp.where(ahead >= 2, 5 - ahead, ahead)
                tiles[p, start:start + rows] = recvs[axis][face, ahead, turn]
        return carry

    lax.fori_loop(0, pairs // 4, take, 0)

    group = 8

    def score_all(h):
        part = slice(h * half, (h + 1) * half)

        def score(i, carry):
            for j in range(group):
                p = i * group + j
                scores = lax.dot_general(
                    lows[h][tile_place(user_tiles[p])], tiles[p], (((1,), (1,)), ((), ())),
                    preferred_element_type=jnp.float32,
                )
                scaled[p] = (weights[p, part].astype(jnp.float32) * scores).astype(jnp.bfloat16)
            return carry

        lax.fori_loop(0, pairs // group, score, 0)

    def spread_all(h, with_rhs):
        part = slice(h * half, (h + 1) * half)

        def spread(i, carry):
            backs = []
            for j in range(group):
                p = i * group + j
                back = jnp.dot(scaled[p], tiles[p], preferred_element_type=jnp.float32)
                if with_rhs:
                    pulled = jnp.dot(
                        pulls[p, part], tiles[p], preferred_element_type=jnp.float32
                    )
                    back = pulled - back
                backs.append(back)
            for j in range(group):
                p = i * group + j
                chain[h, p + 1] = chain[h, table_s[1, p]] + backs[j]
            return carry

        lax.fori_loop(0, pairs // group, spread, 0)

    near, far = (y, x), (x, y)

    def partial(h, t, away, end):
        u = 2 * (end * SIDE + away) if t == 0 else 2 * (away * SIDE + end) + 1
        return chain[h, table_s[2, u]]

    def sum_first(h, t, k):
        to = mesh_id(moved(place, 1 - t, k), core)
        return [
            remote(
                src.at[h, t, k], dst.at[h, t, k], first_sems.at[0, i, h, t, k],
                first_sems.at[1, i, h, t, k], to,
            )
            for i, (src, dst) in enumerate(((part_u, first_u), (part_q, first_q)))
        ]

    def sum_second(h, t, m):
        to = mesh_id(moved(place, t, m), core)
        return [
            remote(
                src.at[h, t, m], dst.at[h, t, m], second_sems.at[0, i, h, t, m],
                second_sems.at[1, i, h, t, m], to,
            )
            for i, (src, dst) in enumerate(((sum_u, second_u), (sum_q, second_q)))
        ]

    def reduce_begin(h):
        for k, t in every:
            for m in range(SIDE):
                whole, unit = quantize(
                    partial(h, t, (near[t] + k) % SIDE, (far[t] + m) % SIDE)
                )
                part_q[h, t, k, m] = whole
                part_u[h, t, k, m] = unit
            for copy in sum_first(h, t, k):
                copy.start()

    def reduce_onward(h):
        for k, t in every:
            for copy in sum_first(h, t, k):
                copy.wait()
        for m in (1, 3, 2, 0):
            for t in range(2):
                total = partial(h, t, near[t], (far[t] + m) % SIDE)
                for k in range(1, SIDE):
                    total = total + restore(first_q[h, t, k, m], first_u[h, t, k, m])
                if m == 0:
                    sums[h, t] = total
                else:
                    whole, unit = quantize(total)
                    sum_q[h, t, m] = whole
                    sum_u[h, t, m] = unit
                    for copy in sum_second(h, t, m):
                        copy.start()

    def reduce_end(h):
        totals = []
        for t in range(2):
            total = sums[h, t]
            for m in range(1, SIDE):
                for copy in sum_second(h, t, m):
                    copy.wait()
                total = total + restore(second_q[h, t, m], second_u[h, t, m])
            totals.append(total)
        return jnp.concatenate(totals, axis=0)

    def gram_term(vectors):
        return (
            jnp.dot(vectors, gram_c[...].reshape(rank, rank), precision=lax.Precision.HIGHEST,
                    preferred_element_type=jnp.float32)
            + REG * vectors
        )

    def row_sum(left, right):
        return jnp.sum(left * right, axis=1, keepdims=True)

    def products(with_rhs):
        score_all(0)
        if not with_rhs:
            gather_onward(1)
        spread_all(0, with_rhs)
        reduce_begin(0)
        if not with_rhs:
            gather_end(1)
        score_all(1)
        reduce_onward(0)
        spread_all(1, with_rhs)
        reduce_begin(1)

    def launch(h, vectors):
        lower(h, vectors)
        gather_begin(h)
        local[h] = gram_term(vectors)

    norms = []
    out[...] = prior[...]
    for h in range(2):
        local[h] = gram_term(half_rows(prior, h))
    products(True)
    for h in range(2):
        if h == 1:
            reduce_onward(1)
            gather_onward(0)
        start = reduce_end(h) - local[h]
        residual[h] = start
        direction[h] = start
        norms.append(row_sum(start, start))
        launch(h, start)

    def iterate(step, norms):
        more = step < ITERS - 1
        gather_end(0)
        products(False)
        fresh = []
        for h in range(2):
            if h == 1:
                reduce_onward(1)
                pl.when(more)(functools.partial(gather_onward, 0))
            image = local[h] + reduce_end(h)
            d = direction[h]
            alpha = norms[h] / (row_sum(d, image) + EPS)
            for t in range(2):
                rows = slice(t * tile + h * half, t * tile + (h + 1) * half)
                block = slice(t * half, (t + 1) * half)
                out[rows] = out[rows] + alpha[block] * d[block]
            r = residual[h] - alpha * image
            residual[h] = r
            fresh.append(row_sum(r, r))
            after = r + fresh[h] / (norms[h] + EPS) * d
            direction[h] = after
            pl.when(more)(functools.partial(launch, h, after))

        return tuple(fresh)

    lax.fori_loop(0, ITERS, iterate, tuple(norms))


def body(user_prior, item_factors, user_tiles, item_tiles, counts):
    n_blk = lax.axis_size("blk")
    n_grp = lax.axis_size("grp")
    n_all = n_blk * n_grp
    pairs, tile, _ = counts.shape
    rank = item_factors.shape[1]
    users = 2 * n_grp
    own = user_prior.shape[0]
    held = item_factors.shape[0] // tile
    half = tile // 2
    grows = rank // n_grp
    vmem = pl.BlockSpec(memory_space=pltpu.VMEM)
    smem = pl.BlockSpec(memory_space=pltpu.SMEM)
    dma = pltpu.SemaphoreType.DMA
    low_type, whole_type, full = jnp.bfloat16, jnp.int16, jnp.float32
    return pl.pallas_call(
        functools.partial(kernel, n_blk, n_grp),
        out_shape=jax.ShapeDtypeStruct((own, rank), full),
        in_specs=[smem, smem, vmem, vmem, pl.BlockSpec(memory_space=pl.ANY)],
        out_specs=vmem,
        scratch_shapes=[
            pltpu.VMEM((1, 128), jnp.int32),
            pltpu.VMEM((n_all, 1, 128), jnp.int32),
            pltpu.SMEM((n_all, 1, 128), jnp.int32),
            pltpu.VMEM((8, 128), jnp.int32),
            pltpu.SMEM((8, 128), jnp.int32),
            *(pltpu.VMEM((CLOSE, held, rows, rank), low_type) for _, rows in SHARE),
            *(pltpu.VMEM((held, rows, rank), low_type) for _, rows in SHARE),
            *(pltpu.VMEM((FACE, SIDE, 2, rows, rank), low_type) for _, rows in SHARE),
            *(pltpu.VMEM((FACE, SIDE, 2, rows, rank), low_type) for _, rows in SHARE),
            pltpu.VMEM((pairs, tile, rank), low_type),
            pltpu.VMEM((pairs, tile, tile), jnp.int32),
            pltpu.VMEM((pairs, tile, tile), low_type),
            pltpu.VMEM((pairs, tile, tile), low_type),
            pltpu.VMEM((pairs, half, tile), low_type),
            pltpu.VMEM((users, half, rank), low_type),
            pltpu.VMEM((users, half, rank), low_type),
            pltpu.VMEM((2, pairs + 1, half, rank), full),
            pltpu.VMEM((n_grp, grows, rank), full),
            pltpu.VMEM((n_grp, grows, rank), full),
            pltpu.VMEM((n_blk, grows, rank), full),
            pltpu.VMEM((n_grp, grows, rank), full),
            pltpu.VMEM((2, grows, rank), full),
            pltpu.VMEM((2, 2, SIDE, SIDE, half, rank), whole_type),
            pltpu.VMEM((2, 2, SIDE, SIDE, 1, rank), full),
            pltpu.VMEM((2, 2, SIDE, SIDE, half, rank), whole_type),
            pltpu.VMEM((2, 2, SIDE, SIDE, 1, rank), full),
            pltpu.VMEM((2, 2, SIDE, half, rank), whole_type),
            pltpu.VMEM((2, 2, SIDE, 1, rank), full),
            pltpu.VMEM((2, 2, SIDE, half, rank), whole_type),
            pltpu.VMEM((2, 2, SIDE, 1, rank), full),
            pltpu.VMEM((2, 2, half, rank), full),
            pltpu.VMEM((2, tile, rank), full),
            pltpu.VMEM((2, tile, rank), full),
            pltpu.VMEM((2, tile, rank), full),
            dma((2, PEERS + 1)),
            dma((2, 3, 4)),
            dma((2, 2, 3, FACE)),
            dma((2, 2, 2, SIDE)),
            dma((2, 2, 2, SIDE)),
            dma((2, 2, 2, 2, SIDE)),
            dma((2, 2, 2, 2, SIDE)),
            dma((3, 2, n_grp)),
            dma((3,)),
        ],
        compiler_params=pltpu.CompilerParams(
            collective_id=0, has_side_effects=True, vmem_limit_bytes=60 << 20
        ),
        name="als",
    )(item_tiles, user_tiles, item_factors.reshape(held, tile, rank), user_prior, counts)


def solution(mesh):
    in_specs = (
        P(("blk", "grp"), None),
        P(("blk", "grp"), None),
        P(("blk", "grp")),
        P(("blk", "grp")),
        P(("blk", "grp"), None, None),
    )
    out_specs = P(("blk", "grp"), None)
    return jax.shard_map(body, mesh=mesh, in_specs=in_specs, out_specs=out_specs, check_vma=False)
```

```python
import functools

import jax
import jax.numpy as jnp
from jax import lax
from jax.experimental import pallas as pl
from jax.experimental.pallas import tpu as pltpu
from jax.sharding import PartitionSpec as P

ITERS = 3
ALPHA = 40.0
REG = 32.0
EPS = 1e-06
SIDE = 4
PLANE = SIDE * SIDE
FACE = 2 * PLANE
PEERS = 73
SLOTS = 2 * SIDE
LEVELS = 32700.0
SHARE = ((0, 48), (48, 48), (96, 32))
AROUND = (0, 1, 3, 2)
CLOSE = 3
SHIFTS = (1, 3, 4, 12, 2, 8, 5, 15, 7, 13, 6, 14, 9, 11, 10)
MESH = pl.DeviceIdType.MESH


def position():
    b = lax.axis_index("blk")
    g = lax.axis_index("grp")
    return (g // SIDE, g % SIDE, b // 2), b % 2


def mesh_id(place, core):
    x, y, z = place
    return z * 2 + core, x * SIDE + y


def flat_id(place, core):
    b, g = mesh_id(place, core)
    return b * PLANE + g


def moved(place, axis, k):
    return tuple((v + k) % SIDE if i == axis else v for i, v in enumerate(place))


def put_at(place, axis, value):
    return tuple(value if i == axis else v for i, v in enumerate(place))


def remote(src, dst, send_sem, recv_sem, device):
    return pltpu.make_async_remote_copy(
        src_ref=src, dst_ref=dst, send_sem=send_sem, recv_sem=recv_sem,
        device_id=device, device_id_type=MESH,
    )


def quantize(value):
    top = jnp.maximum(jnp.max(jnp.abs(value), axis=0, keepdims=True), 1e-30)
    whole = jnp.round(value * (LEVELS / top)).astype(jnp.int32).astype(jnp.int16)
    return whole, top * (1.0 / LEVELS)


def restore(whole, unit):
    return whole.astype(jnp.int32).astype(jnp.float32) * unit


def tile_place(u):
    g = u // 2
    x, y = g // SIDE, g % SIDE
    return jnp.where(u % 2 == 0, y * SIDE + x, PLANE + x * SIDE + y)


def kernel(
    n_blk, n_grp,
    wanted_tiles, user_tiles, items, prior, counts,
    out,
    req, reqs, want, table, table_s,
    ring0, ring1, ring2, far0, far1, far2, send0, send1, send2, recv0, recv1, recv2,
    tiles, counted, weights, pulls, scaled, low0, low1, chain,
    gram_own, gram_a, gram_b, gram_c, gram_t,
    part_q, part_u, first_q, first_u, sum_q, sum_u, second_q, second_u, sums,
    residual, direction, local,
    req_sems, ring_sems, tile_sems, gather_one, gather_two, first_sems, second_sems,
    gram_sems, local_sems,
):
    n_all = n_blk * n_grp
    place, core = position()
    x, y, z = place
    b, g = mesh_id(place, core)
    me = b * n_grp + g
    pairs, tile, rank = tiles.shape
    held = items.shape[0]
    half = tile // 2
    fars = (far0, far1, far2)
    lows = (low0, low1)
    rings, sends, recvs = (ring0, ring1, ring2), (send0, send1, send2), (recv0, recv1, recv2)

    def half_rows(ref, h):
        return jnp.concatenate(
            [ref[t * tile + h * half:t * tile + (h + 1) * half] for t in range(2)], axis=0
        )

    def lower(h, vectors):
        d_low = vectors.astype(jnp.bfloat16)
        lows[h][y * SIDE + x] = d_low[:half]
        lows[h][PLANE + x * SIDE + y] = d_low[half:]

    count_copy = pltpu.make_async_copy(counts, counted, local_sems.at[0])
    count_copy.start()

    def same_x(i):
        return (place[0], (y + i // 8) % SIDE, (z + i // 2) % SIDE), (core + i) % 2

    def same_y(i):
        return ((x + 1 + i // 8) % SIDE, place[1], (z + i // 2) % SIDE), (core + i) % 2

    def same_z(i):
        return ((x + 1 + i // 2 % 3) % SIDE, (y + 1 + i // 6) % SIDE, place[2]), (core + i) % 2

    families = ((same_x, 1, 32, 0), (same_y, 0, 24, 32), (same_z, 0, 18, 56))

    def for_peers(act):
        for family, first, last, base in families:
            def one(i, carry):
                act(mesh_id(*family(i)), base + i)
                return carry

            lax.fori_loop(first, last, one, 0)

    barrier = pltpu.get_barrier_semaphore()
    for_peers(
        lambda to, i: pl.semaphore_signal(barrier, inc=1, device_id=to, device_id_type=MESH)
    )

    lane = lax.broadcasted_iota(jnp.int32, (1, 128), 1)
    zero = jnp.zeros((1, 128), jnp.int32)

    def ask(i, state):
        first, second = state
        for j in range(8):
            p = i * 8 + j
            late, early = wanted_tiles[p], wanted_tiles[pairs - 1 - p]
            second = jnp.where(lane == late // held, late % held, second)
            first = jnp.where(lane == early // held, early % held, first)
        return first, second

    first, second = lax.fori_loop(0, pairs // 8, ask, (zero, zero))
    asked = first + 256 * second
    req[...] = asked
    reqs[me] = asked
    for h in range(2):
        lower(h, half_rows(prior, h))

    def keep(i, carry):
        for axis, (start, rows) in enumerate(SHARE):
            rings[axis][0, i] = items[i, start:start + rows]
        return carry

    lax.fori_loop(0, held, keep, 0)

    pl.semaphore_wait(barrier, PEERS)

    def request(to, i):
        return remote(req, reqs.at[me], req_sems.at[0, i], req_sems.at[1, i], to)

    for_peers(lambda to, i: request(to, i).start())

    def ring_copy(axis, kind):
        start, rows = SHARE[axis]
        source = 2 if kind % 2 == 0 else 1
        if kind < 2:
            src, dst = items.at[:, pl.ds(start, rows)], rings[axis].at[source]
        else:
            half = pl.ds(0 if kind == 2 else held // 2, held // 2)
            src, dst = rings[axis].at[source, half], fars[axis].at[half]
        to = moved(place, axis, 1 if kind % 2 == 0 else SIDE - 1)
        return remote(
            src, dst, ring_sems.at[0, axis, kind], ring_sems.at[1, axis, kind],
            mesh_id(to, core),
        )

    for kind in range(2):
        for axis in range(3):
            ring_copy(axis, kind).start()

    def low_place(t, m):
        if t == 0:
            return y * SIDE + (x + SIDE - m) % SIDE
        return PLANE + x * SIDE + (y + SIDE - m) % SIDE

    def gather_a(h, t, k):
        ref = lows[h].at[low_place(t, 0)]
        return remote(
            ref, ref, gather_one.at[0, h, t, k], gather_one.at[1, h, t, k],
            mesh_id(moved(place, t, k), core),
        )

    def gather_b(h, t, k, m):
        ref = lows[h].at[low_place(t, m)]
        return remote(
            ref, ref, gather_two.at[0, h, t, k, m], gather_two.at[1, h, t, k, m],
            mesh_id(moved(place, 1 - t, k), core),
        )

    def gather_begin(h):
        for k in range(1, SIDE):
            for t in range(2):
                gather_a(h, t, k).start()
        for k in range(1, SIDE):
            for t in range(2):
                gather_b(h, t, k, 0).start()

    def gather_onward(h):
        for m in range(1, SIDE):
            for t in range(2):
                gather_a(h, t, m).wait()
                for k in range(1, SIDE):
                    gather_b(h, t, k, m).start()

    def gather_end(h):
        for m in range(SIDE):
            for k in range(1, SIDE):
                for t in range(2):
                    gather_b(h, t, k, m).wait()

    gather_begin(0)
    gather_begin(1)

    chunk = min(8, held)

    def gram_step(i, total):
        block = items[pl.ds(i * chunk, chunk)].reshape(chunk * tile, rank)
        return total + lax.dot_general(
            block, block, (((0,), (0,)), ((), ())), preferred_element_type=jnp.float32
        )

    gram_own[...] = lax.fori_loop(
        0, held // chunk, gram_step, jnp.zeros((rank, rank), jnp.float32)
    ).reshape(n_grp, rank // n_grp, rank)

    def gram_first(k):
        to = (g + k) % n_grp
        return remote(
            gram_own.at[to], gram_a.at[k], gram_sems.at[0, 0, k], gram_sems.at[0, 1, k], (b, to)
        )

    def gram_second(k):
        return remote(
            gram_t.at[0], gram_b.at[k], gram_sems.at[1, 0, k], gram_sems.at[1, 1, k],
            ((b + k) % n_blk, g),
        )

    def gram_third(k):
        return remote(
            gram_t.at[1], gram_c.at[g], gram_sems.at[2, 0, k], gram_sems.at[2, 1, k],
            (b, (g + k) % n_grp),
        )

    for k in range(1, n_grp):
        gram_first(k).start()

    for_peers(lambda to, i: request(to, i).wait())
    want_copy = pltpu.make_async_copy(reqs, want, local_sems.at[1])
    want_copy.start()
    for axis in range(3):
        for kind in range(2):
            ring_copy(axis, kind).wait()
            ring_copy(axis, kind + 2).start()
    want_copy.wait()

    def face_shift(turn):
        words = [sum(v << 4 * j for j, v in enumerate(SHIFTS[i:i + 7])) for i in (0, 7, 14)]
        last = turn >= 28
        i = jnp.where(last, 14, turn // 4 * 2 + turn % 2)
        flip = jnp.where(last, turn % 2, turn // 2 % 2)
        word = jnp.where(i < 7, words[0], jnp.where(i < 14, words[1], words[2]))
        shift = lax.shift_right_logical(jnp.int32(word), 4 * (i % 7)) % 16
        return shift * 2 + flip

    def face_target(axis, step):
        a, c = step // 2 // SIDE, step // 2 % SIDE
        a = jnp.where(core == 0, a, (SIDE - a) % SIDE)
        c = jnp.where(core == 0, c, (SIDE - c) % SIDE)
        to = moved(moved(place, (axis + 1) % 3, a), (axis + 2) % 3, c)
        return to, (core + step) % 2

    def face_index(axis):
        return (place[(axis + 1) % 3] * SIDE + place[(axis + 2) % 3]) * 2 + core

    def pack_into(ref, slot, axis, to, which):
        for i in which:
            w = (place[axis] + AROUND[i]) % SIDE
            pair = want[to, 0, flat_id(put_at(place, axis, w), core)]
            for j, held_at in enumerate((pair % 256, pair // 256)):
                ref[slot * SLOTS + 2 * i + j] = rings[axis][i, held_at] if i < CLOSE else fars[axis][held_at]

    levels = (tuple(range(CLOSE)), tuple(range(CLOSE, SIDE)))

    def pack(level, step):
        for axis in range(3):
            to, to_core = face_target(axis, step)
            pack_into(sends[axis], step, axis, flat_id(to, to_core), levels[level])

    def parcel(level, axis, step):
        to, to_core = face_target(axis, step)
        start, size = 2 * levels[level][0], 2 * len(levels[level])
        return remote(
            sends[axis].at[pl.ds(step * SLOTS + start, size)],
            recvs[axis].at[pl.ds(face_index(axis) * SLOTS + start, size)],
            tile_sems.at[0, level, axis, step], tile_sems.at[1, level, axis, step],
            mesh_id(to, to_core),
        )

    def ship(level, first, last):
        pack(level, face_shift(first))

        def one(turn, carry):
            pack(level, face_shift(turn + 1))
            for axis in range(3):
                parcel(level, axis, face_shift(turn)).start()
            return carry

        lax.fori_loop(first, last - 1, one, 0)
        for axis in range(3):
            parcel(level, axis, face_shift(last - 1)).start()

    turns_all = 2 * len(SHIFTS)
    ship(0, 0, 4)
    gather_onward(0)
    gather_onward(1)
    for k in range(1, n_grp):
        gram_first(k).wait()
    part = gram_own[g]
    for k in range(1, n_grp):
        part = part + gram_a[k]
    gram_t[0] = part
    ship(0, 4, 16)
    for k in range(1, n_blk):
        gram_second(k).start()
    ship(0, 16, turns_all)
    for k in range(1, n_blk):
        gram_second(k).wait()
    part = gram_t[0]
    for k in range(1, n_blk):
        part = part + gram_b[k]
    gram_t[1] = part
    gram_c[g] = part
    for axis in range(3):
        for kind in range(2, 4):
            ring_copy(axis, kind).wait()
    pack(0, 1)
    pack(1, 1)
    ship(1, 0, turns_all)
    for level in range(2):
        for axis in range(3):
            parcel(level, axis, 1).start()
    for k in range(1, n_grp):
        gram_third(k).start()
    for axis in range(3):
        pack_into(recvs[axis], face_index(axis), axis, me, range(SIDE))

    def link(p, state):
        seen, order, last, before, users_of = state
        owner = wanted_tiles[p] // held
        hit = lane == owner
        turn = jnp.sum(jnp.where(hit, seen, 0), axis=1, keepdims=True)
        order = jnp.where(lane == p, owner * 2 + jnp.minimum(turn, 1), order)
        seen = jnp.where(hit, 1, seen)
        mine = lane == user_tiles[p]
        earlier = jnp.sum(jnp.where(mine, last, 0), axis=1, keepdims=True)
        before = jnp.where(lane == p, earlier, before)
        last = jnp.where(mine, p + 1, last)
        users_of = jnp.where(lane == p, user_tiles[p], users_of)
        return seen, order, last, before, users_of

    _, order, last, before, users_of = lax.fori_loop(0, pairs, link, (zero,) * 5)
    owner = order // 2
    owner_b, owner_g = owner // n_grp, owner % n_grp
    at, of = (owner_g // SIDE, owner_g % SIDE, owner_b // 2), owner_b % 2
    table[...] = jnp.zeros((8, 128), jnp.int32)
    table[1:2] = before
    table[2:3] = last
    table[3:4] = tile_place(users_of)
    for axis in range(3):
        face = (at[(axis + 1) % 3] * SIDE + at[(axis + 2) % 3]) * 2 + of
        ahead = (at[axis] + SIDE - place[axis]) % SIDE
        ahead = jnp.where(ahead >= 2, 5 - ahead, ahead)
        table[4 + axis:5 + axis] = face * SLOTS + ahead * 2 + order % 2
    table_copy = pltpu.make_async_copy(table, table_s, local_sems.at[2])
    table_copy.start()
    count_copy.wait()

    def weigh(p, carry):
        weight = counted[p].astype(jnp.float32) * ALPHA
        weights[p] = weight.astype(jnp.bfloat16)
        pulls[p] = jnp.where(weight > 0, 1.0 + weight, 0.0).astype(jnp.bfloat16)
        return carry

    lax.fori_loop(0, pairs, weigh, 0)
    for h in range(2):
        chain[h, 0] = jnp.zeros((half, rank), jnp.float32)
    table_copy.wait()

    gather_end(0)
    gather_end(1)
    for k in range(1, n_grp):
        gram_third(k).wait()

    def wait_parcel(step, carry):
        for level in range(2):
            for axis in range(3):
                parcel(level, axis, step).wait()
        return carry

    lax.fori_loop(1, FACE, wait_parcel, 0)

    def take(i, carry):
        for j in range(4):
            p = i * 4 + j
            for axis, (start, rows) in enumerate(SHARE):
                tiles[p, start:start + rows] = recvs[axis][table_s[4 + axis, p]]
        return carry

    lax.fori_loop(0, pairs // 4, take, 0)

    group = 8

    def score_all(h):
        part = slice(h * half, (h + 1) * half)

        def score(i, carry):
            for j in range(group):
                p = i * group + j
                scores = lax.dot_general(
                    lows[h][table_s[3, p]], tiles[p], (((1,), (1,)), ((), ())),
                    preferred_element_type=jnp.float32,
                )
                scaled[p, :half] = (weights[p, part].astype(jnp.float32) * scores).astype(jnp.bfloat16)
            return carry

        lax.fori_loop(0, pairs // group, score, 0)

    def spread_all(h):
        def spread(i, carry):
            backs = [
                jnp.dot(scaled[p, :half], tiles[p], preferred_element_type=jnp.float32)
                for p in (i * group + j for j in range(group))
            ]
            for j in range(group):
                p = i * group + j
                chain[h, p + 1] = chain[h, table_s[1, p]] + backs[j]
            return carry

        lax.fori_loop(0, pairs // group, spread, 0)

    def first_products():
        def score(i, carry):
            for j in range(group):
                p = i * group + j
                at = table_s[3, p]
                scores = lax.dot_general(
                    jnp.concatenate([lows[0][at], lows[1][at]], axis=0), tiles[p],
                    (((1,), (1,)), ((), ())), preferred_element_type=jnp.float32,
                )
                scaled[p] = (weights[p].astype(jnp.float32) * scores).astype(jnp.bfloat16)
            return carry

        lax.fori_loop(0, pairs // group, score, 0)

        def spread(i, carry):
            backs = []
            for j in range(group // 2):
                p = i * (group // 2) + j
                backs.append(
                    jnp.dot(pulls[p], tiles[p], preferred_element_type=jnp.float32)
                    - jnp.dot(scaled[p], tiles[p], preferred_element_type=jnp.float32)
                )
            for j in range(group // 2):
                p = i * (group // 2) + j
                for h in range(2):
                    part = backs[j][h * half:(h + 1) * half]
                    chain[h, p + 1] = chain[h, table_s[1, p]] + part
            return carry

        lax.fori_loop(0, pairs // (group // 2), spread, 0)

    near, far = (y, x), (x, y)

    def partial(h, t, away, end):
        u = 2 * (end * SIDE + away) if t == 0 else 2 * (away * SIDE + end) + 1
        return chain[h, table_s[2, u]]

    def sum_first(h, t, k, m):
        to = mesh_id(moved(place, 1 - t, k), core)
        return [
            remote(
                src.at[h, t, k, m], dst.at[h, t, k, m], first_sems.at[0, i, h, t, k, m],
                first_sems.at[1, i, h, t, k, m], to,
            )
            for i, (src, dst) in enumerate(((part_u, first_u), (part_q, first_q)))
        ]

    def sum_second(h, t, m):
        to = mesh_id(moved(place, t, m), core)
        return [
            remote(
                src.at[h, t, m], dst.at[h, t, m], second_sems.at[0, i, h, t, m],
                second_sems.at[1, i, h, t, m], to,
            )
            for i, (src, dst) in enumerate(((sum_u, second_u), (sum_q, second_q)))
        ]

    turns = tuple(range(1, SIDE)) + (0,)

    def reduce_begin(h):
        for m in turns:
            for k in range(1, SIDE):
                for t in range(2):
                    whole, unit = quantize(
                        partial(h, t, (near[t] + k) % SIDE, (far[t] + m) % SIDE)
                    )
                    part_q[h, t, k, m] = whole
                    part_u[h, t, k, m] = unit
                    for copy in sum_first(h, t, k, m):
                        copy.start()

    def reduce_onward(h):
        for m in turns:
            for t in range(2):
                total = partial(h, t, near[t], (far[t] + m) % SIDE)
                for k in range(1, SIDE):
                    for copy in sum_first(h, t, k, m):
                        copy.wait()
                    total = total + restore(first_q[h, t, k, m], first_u[h, t, k, m])
                if m == 0:
                    sums[h, t] = total
                else:
                    whole, unit = quantize(total)
                    sum_q[h, t, m] = whole
                    sum_u[h, t, m] = unit
                    for copy in sum_second(h, t, m):
                        copy.start()

    def reduce_end(h):
        totals = []
        for t in range(2):
            total = sums[h, t]
            for m in range(1, SIDE):
                for copy in sum_second(h, t, m):
                    copy.wait()
                total = total + restore(second_q[h, t, m], second_u[h, t, m])
            totals.append(total)
        return jnp.concatenate(totals, axis=0)

    def gram_term(vectors):
        return (
            jnp.dot(vectors, gram_c[...].reshape(rank, rank), precision=lax.Precision.HIGHEST,
                    preferred_element_type=jnp.float32)
            + REG * vectors
        )

    def row_sum(left, right):
        return jnp.sum(left * right, axis=1, keepdims=True)

    def products():
        score_all(0)
        gather_onward(1)
        spread_all(0)
        reduce_begin(0)
        gather_end(1)
        score_all(1)
        reduce_onward(0)
        spread_all(1)
        reduce_begin(1)

    def launch(h, vectors):
        lower(h, vectors)
        gather_begin(h)
        local[h] = gram_term(vectors)

    norms = []
    out[...] = prior[...]
    first_products()
    for h in range(2):
        reduce_begin(h)
    for h in range(2):
        local[h] = gram_term(half_rows(prior, h))
    reduce_onward(0)
    for h in range(2):
        if h == 1:
            reduce_onward(1)
            gather_onward(0)
        start = reduce_end(h) - local[h]
        residual[h] = start
        direction[h] = start
        norms.append(row_sum(start, start))
        launch(h, start)

    def iterate(step, norms):
        more = step < ITERS - 1
        gather_end(0)
        products()
        fresh = []
        for h in range(2):
            if h == 1:
                reduce_onward(1)
                pl.when(more)(functools.partial(gather_onward, 0))
            image = local[h] + reduce_end(h)
            d = direction[h]
            alpha = norms[h] / (row_sum(d, image) + EPS)
            for t in range(2):
                rows = slice(t * tile + h * half, t * tile + (h + 1) * half)
                block = slice(t * half, (t + 1) * half)
                out[rows] = out[rows] + alpha[block] * d[block]
            r = residual[h] - alpha * image
            residual[h] = r
            fresh.append(row_sum(r, r))
            after = r + fresh[h] / (norms[h] + EPS) * d
            direction[h] = after
            pl.when(more)(functools.partial(launch, h, after))

        return tuple(fresh)

    lax.fori_loop(0, ITERS, iterate, tuple(norms))


def body(user_prior, item_factors, user_tiles, item_tiles, counts):
    n_blk = lax.axis_size("blk")
    n_grp = lax.axis_size("grp")
    n_all = n_blk * n_grp
    pairs, tile, _ = counts.shape
    rank = item_factors.shape[1]
    users = 2 * n_grp
    own = user_prior.shape[0]
    held = item_factors.shape[0] // tile
    half = tile // 2
    grows = rank // n_grp
    vmem = pl.BlockSpec(memory_space=pltpu.VMEM)
    smem = pl.BlockSpec(memory_space=pltpu.SMEM)
    dma = pltpu.SemaphoreType.DMA
    low_type, whole_type, full = jnp.bfloat16, jnp.int16, jnp.float32
    return pl.pallas_call(
        functools.partial(kernel, n_blk, n_grp),
        out_shape=jax.ShapeDtypeStruct((own, rank), full),
        in_specs=[smem, smem, vmem, vmem, pl.BlockSpec(memory_space=pl.ANY)],
        out_specs=vmem,
        scratch_shapes=[
            pltpu.VMEM((1, 128), jnp.int32),
            pltpu.VMEM((n_all, 1, 128), jnp.int32),
            pltpu.SMEM((n_all, 1, 128), jnp.int32),
            pltpu.VMEM((8, 128), jnp.int32),
            pltpu.SMEM((8, 128), jnp.int32),
            *(pltpu.VMEM((CLOSE, held, rows, rank), low_type) for _, rows in SHARE),
            *(pltpu.VMEM((held, rows, rank), low_type) for _, rows in SHARE),
            *(pltpu.VMEM((FACE * SLOTS, rows, rank), low_type) for _, rows in SHARE),
            *(pltpu.VMEM((FACE * SLOTS, rows, rank), low_type) for _, rows in SHARE),
            pltpu.VMEM((pairs, tile, rank), low_type),
            pltpu.VMEM((pairs, tile, tile), jnp.int32),
            pltpu.VMEM((pairs, tile, tile), low_type),
            pltpu.VMEM((pairs, tile, tile), low_type),
            pltpu.VMEM((pairs, tile, tile), low_type),
            pltpu.VMEM((users, half, rank), low_type),
            pltpu.VMEM((users, half, rank), low_type),
            pltpu.VMEM((2, pairs + 1, half, rank), full),
            pltpu.VMEM((n_grp, grows, rank), full),
            pltpu.VMEM((n_grp, grows, rank), full),
            pltpu.VMEM((n_blk, grows, rank), full),
            pltpu.VMEM((n_grp, grows, rank), full),
            pltpu.VMEM((2, grows, rank), full),
            pltpu.VMEM((2, 2, SIDE, SIDE, half, rank), whole_type),
            pltpu.VMEM((2, 2, SIDE, SIDE, 1, rank), full),
            pltpu.VMEM((2, 2, SIDE, SIDE, half, rank), whole_type),
            pltpu.VMEM((2, 2, SIDE, SIDE, 1, rank), full),
            pltpu.VMEM((2, 2, SIDE, half, rank), whole_type),
            pltpu.VMEM((2, 2, SIDE, 1, rank), full),
            pltpu.VMEM((2, 2, SIDE, half, rank), whole_type),
            pltpu.VMEM((2, 2, SIDE, 1, rank), full),
            pltpu.VMEM((2, 2, half, rank), full),
            pltpu.VMEM((2, tile, rank), full),
            pltpu.VMEM((2, tile, rank), full),
            pltpu.VMEM((2, tile, rank), full),
            dma((2, PEERS + 1)),
            dma((2, 3, 4)),
            dma((2, 2, 3, FACE)),
            dma((2, 2, 2, SIDE)),
            dma((2, 2, 2, SIDE, SIDE)),
            dma((2, 2, 2, 2, SIDE, SIDE)),
            dma((2, 2, 2, 2, SIDE)),
            dma((3, 2, n_grp)),
            dma((3,)),
        ],
        compiler_params=pltpu.CompilerParams(
            collective_id=0, has_side_effects=True, vmem_limit_bytes=60 << 20
        ),
        name="als",
    )(item_tiles, user_tiles, item_factors.reshape(held, tile, rank), user_prior, counts)


def solution(mesh):
    in_specs = (
        P(("blk", "grp"), None),
        P(("blk", "grp"), None),
        P(("blk", "grp")),
        P(("blk", "grp")),
        P(("blk", "grp"), None, None),
    )
    out_specs = P(("blk", "grp"), None)
    return jax.shard_map(body, mesh=mesh, in_specs=in_specs, out_specs=out_specs, check_vma=False)
```

```python
import functools

import jax
import jax.numpy as jnp
from jax import lax
from jax.experimental import pallas as pl
from jax.experimental.pallas import tpu as pltpu
from jax.sharding import PartitionSpec as P

ITERS = 3
ALPHA = 40.0
REG = 32.0
EPS = 1e-06
SIDE = 4
PLANE = SIDE * SIDE
FACE = 2 * PLANE
PEERS = 73
SLOTS = 2 * SIDE
LEVELS = 32700.0
SHARE = ((0, 48), (48, 48), (96, 32))
AROUND = (0, 1, 3, 2)
CLOSE = 3
SHIFTS = (1, 3, 4, 12, 2, 8, 5, 15, 7, 13, 6, 14, 9, 11, 10)
MESH = pl.DeviceIdType.MESH


def position():
    b = lax.axis_index("blk")
    g = lax.axis_index("grp")
    return (g // SIDE, g % SIDE, b // 2), b % 2


def mesh_id(place, core):
    x, y, z = place
    return z * 2 + core, x * SIDE + y


def flat_id(place, core):
    b, g = mesh_id(place, core)
    return b * PLANE + g


def moved(place, axis, k):
    return tuple((v + k) % SIDE if i == axis else v for i, v in enumerate(place))


def put_at(place, axis, value):
    return tuple(value if i == axis else v for i, v in enumerate(place))


def remote(src, dst, send_sem, recv_sem, device):
    return pltpu.make_async_remote_copy(
        src_ref=src, dst_ref=dst, send_sem=send_sem, recv_sem=recv_sem,
        device_id=device, device_id_type=MESH,
    )


def quantize(value):
    top = jnp.maximum(jnp.max(jnp.abs(value), axis=0, keepdims=True), 1e-30)
    whole = jnp.round(value * (LEVELS / top)).astype(jnp.int32).astype(jnp.int16)
    return whole, top * (1.0 / LEVELS)


def restore(whole, unit):
    return whole.astype(jnp.int32).astype(jnp.float32) * unit


def tile_place(u):
    g = u // 2
    x, y = g // SIDE, g % SIDE
    return jnp.where(u % 2 == 0, y * SIDE + x, PLANE + x * SIDE + y)


def kernel(
    n_blk, n_grp,
    wanted_tiles, user_tiles, items, prior, counts,
    out,
    req, reqs, want, table, table_s,
    ring0, ring1, ring2, far0, far1, far2, send0, send1, send2, recv0, recv1, recv2,
    tiles, counted, weights, pulls, scaled, low0, low1, chain,
    gram_own, gram_a, gram_b, gram_c, gram_t,
    part_q, part_u, first_q, first_u, sum_q, sum_u, second_q, second_u, sums,
    residual, direction, local,
    req_sems, ring_sems, tile_sems, gather_one, gather_two, first_sems, second_sems,
    gram_sems, local_sems,
):
    n_all = n_blk * n_grp
    place, core = position()
    x, y, z = place
    b, g = mesh_id(place, core)
    me = b * n_grp + g
    pairs, tile, rank = tiles.shape
    held = items.shape[0]
    half = tile // 2
    fars = (far0, far1, far2)
    lows = (low0, low1)
    rings, sends, recvs = (ring0, ring1, ring2), (send0, send1, send2), (recv0, recv1, recv2)

    def half_rows(ref, h):
        return jnp.concatenate(
            [ref[t * tile + h * half:t * tile + (h + 1) * half] for t in range(2)], axis=0
        )

    def lower(h, vectors):
        d_low = vectors.astype(jnp.bfloat16)
        lows[h][y * SIDE + x] = d_low[:half]
        lows[h][PLANE + x * SIDE + y] = d_low[half:]

    count_copy = pltpu.make_async_copy(counts, counted, local_sems.at[0])
    count_copy.start()

    xs, ys, zs = ([(v + d) % SIDE for d in range(SIDE)] for v in place)
    planes = [[xs[i] * SIDE + ys[j] for j in range(SIDE)] for i in range(SIDE)]
    stacks = [[zs[k] * 2 + c for c in (core, 1 - core)] for k in range(SIDE)]
    peers = [
        (stacks[k][c], planes[i][j])
        for i in range(SIDE) for j in range(SIDE) for k in range(SIDE) for c in range(2)
        if i * j * k == 0 and i + j + k + c > 0
    ]
    assert len(peers) == PEERS

    def for_peers(act):
        for i, to in enumerate(peers):
            act(to, i)

    barrier = pltpu.get_barrier_semaphore()
    for_peers(
        lambda to, i: pl.semaphore_signal(barrier, inc=1, device_id=to, device_id_type=MESH)
    )

    lane = lax.broadcasted_iota(jnp.int32, (1, 128), 1)
    zero = jnp.zeros((1, 128), jnp.int32)

    def ask(i, state):
        first, second = state
        for j in range(8):
            p = i * 8 + j
            late, early = wanted_tiles[p], wanted_tiles[pairs - 1 - p]
            second = jnp.where(lane == late // held, late % held, second)
            first = jnp.where(lane == early // held, early % held, first)
        return first, second

    first, second = lax.fori_loop(0, pairs // 8, ask, (zero, zero))
    asked = first + 256 * second
    req[...] = asked
    reqs[me] = asked
    for h in range(2):
        lower(h, half_rows(prior, h))

    pl.semaphore_wait(barrier, PEERS)

    def request(to, i):
        return remote(req, reqs.at[me], req_sems.at[0, i], req_sems.at[1, i], to)

    for_peers(lambda to, i: request(to, i).start())

    def ring_copy(axis, kind):
        start, rows = SHARE[axis]
        source = 2 if kind % 2 == 0 else 1
        if kind < 2:
            src, dst = items.at[:, pl.ds(start, rows)], rings[axis].at[source]
        else:
            half = pl.ds(0 if kind == 2 else held // 2, held // 2)
            src, dst = rings[axis].at[source, half], fars[axis].at[half]
        to = moved(place, axis, 1 if kind % 2 == 0 else SIDE - 1)
        return remote(
            src, dst, ring_sems.at[0, axis, kind], ring_sems.at[1, axis, kind],
            mesh_id(to, core),
        )

    for kind in range(2):
        for axis in range(3):
            ring_copy(axis, kind).start()

    def low_place(t, m):
        if t == 0:
            return y * SIDE + (x + SIDE - m) % SIDE
        return PLANE + x * SIDE + (y + SIDE - m) % SIDE

    def gather_a(h, t, k):
        ref = lows[h].at[low_place(t, 0)]
        return remote(
            ref, ref, gather_one.at[0, h, t, k], gather_one.at[1, h, t, k],
            mesh_id(moved(place, t, k), core),
        )

    def gather_b(h, t, k, m):
        ref = lows[h].at[low_place(t, m)]
        return remote(
            ref, ref, gather_two.at[0, h, t, k, m], gather_two.at[1, h, t, k, m],
            mesh_id(moved(place, 1 - t, k), core),
        )

    def gather_begin(h):
        for k in range(1, SIDE):
            for t in range(2):
                gather_a(h, t, k).start()
        for k in range(1, SIDE):
            for t in range(2):
                gather_b(h, t, k, 0).start()

    def gather_onward(h):
        for m in range(1, SIDE):
            for t in range(2):
                gather_a(h, t, m).wait()
                for k in range(1, SIDE):
                    gather_b(h, t, k, m).start()

    def gather_end(h):
        for m in range(SIDE):
            for k in range(1, SIDE):
                for t in range(2):
                    gather_b(h, t, k, m).wait()

    gather_begin(0)
    gather_begin(1)

    def keep(i, carry):
        for axis, (start, rows) in enumerate(SHARE):
            rings[axis][0, i] = items[i, start:start + rows]
        return carry

    lax.fori_loop(0, held, keep, 0)

    chunk = min(8, held)

    def gram_step(i, total):
        block = items[pl.ds(i * chunk, chunk)].reshape(chunk * tile, rank)
        return total + lax.dot_general(
            block, block, (((0,), (0,)), ((), ())), preferred_element_type=jnp.float32
        )

    gram_own[...] = lax.fori_loop(
        0, held // chunk, gram_step, jnp.zeros((rank, rank), jnp.float32)
    ).reshape(n_grp, rank // n_grp, rank)

    def gram_first(k):
        to = (g + k) % n_grp
        return remote(
            gram_own.at[to], gram_a.at[k], gram_sems.at[0, 0, k], gram_sems.at[0, 1, k], (b, to)
        )

    def gram_second(k):
        return remote(
            gram_t.at[0], gram_b.at[k], gram_sems.at[1, 0, k], gram_sems.at[1, 1, k],
            ((b + k) % n_blk, g),
        )

    def gram_third(k):
        return remote(
            gram_t.at[1], gram_c.at[g], gram_sems.at[2, 0, k], gram_sems.at[2, 1, k],
            (b, (g + k) % n_grp),
        )

    for k in range(1, n_grp):
        gram_first(k).start()

    for_peers(lambda to, i: request(to, i).wait())
    want_copy = pltpu.make_async_copy(reqs, want, local_sems.at[1])
    want_copy.start()
    for axis in range(3):
        for kind in range(2):
            ring_copy(axis, kind).wait()
            ring_copy(axis, kind + 2).start()
    want_copy.wait()

    def face_shift(turn):
        words = [sum(v << 4 * j for j, v in enumerate(SHIFTS[i:i + 7])) for i in (0, 7, 14)]
        last = turn >= 28
        i = jnp.where(last, 14, turn // 4 * 2 + turn % 2)
        flip = jnp.where(last, turn % 2, turn // 2 % 2)
        word = jnp.where(i < 7, words[0], jnp.where(i < 14, words[1], words[2]))
        shift = lax.shift_right_logical(jnp.int32(word), 4 * (i % 7)) % 16
        return shift * 2 + flip

    def face_target(axis, step):
        a, c = step // 2 // SIDE, step // 2 % SIDE
        a = jnp.where(core == 0, a, (SIDE - a) % SIDE)
        c = jnp.where(core == 0, c, (SIDE - c) % SIDE)
        to = moved(moved(place, (axis + 1) % 3, a), (axis + 2) % 3, c)
        return to, (core + step) % 2

    def face_index(axis):
        return (place[(axis + 1) % 3] * SIDE + place[(axis + 2) % 3]) * 2 + core

    def pack_into(ref, slot, axis, to, which):
        for i in which:
            w = (place[axis] + AROUND[i]) % SIDE
            pair = want[to, 0, flat_id(put_at(place, axis, w), core)]
            for j, held_at in enumerate((pair % 256, pair // 256)):
                ref[slot * SLOTS + 2 * i + j] = rings[axis][i, held_at] if i < CLOSE else fars[axis][held_at]

    levels = (tuple(range(CLOSE)), tuple(range(CLOSE, SIDE)))

    def pack(level, step):
        for axis in range(3):
            to, to_core = face_target(axis, step)
            pack_into(sends[axis], step, axis, flat_id(to, to_core), levels[level])

    def parcel(level, axis, step):
        to, to_core = face_target(axis, step)
        start, size = 2 * levels[level][0], 2 * len(levels[level])
        return remote(
            sends[axis].at[pl.ds(step * SLOTS + start, size)],
            recvs[axis].at[pl.ds(face_index(axis) * SLOTS + start, size)],
            tile_sems.at[0, level, axis, step], tile_sems.at[1, level, axis, step],
            mesh_id(to, to_core),
        )

    def ship(level, first, last):
        pack(level, face_shift(first))

        def one(turn, carry):
            pack(level, face_shift(turn + 1))
            for axis in range(3):
                parcel(level, axis, face_shift(turn)).start()
            return carry

        lax.fori_loop(first, last - 1, one, 0)
        for axis in range(3):
            parcel(level, axis, face_shift(last - 1)).start()

    turns_all = 2 * len(SHIFTS)
    ship(0, 0, 4)
    gather_onward(0)
    gather_onward(1)
    for k in range(1, n_grp):
        gram_first(k).wait()
    part = gram_own[g]
    for k in range(1, n_grp):
        part = part + gram_a[k]
    gram_t[0] = part
    ship(0, 4, 16)
    for k in range(1, n_blk):
        gram_second(k).start()
    ship(0, 16, turns_all)
    for k in range(1, n_blk):
        gram_second(k).wait()
    part = gram_t[0]
    for k in range(1, n_blk):
        part = part + gram_b[k]
    gram_t[1] = part
    gram_c[g] = part
    for axis in range(3):
        for kind in range(2, 4):
            ring_copy(axis, kind).wait()
    pack(0, 1)
    pack(1, 1)
    ship(1, 0, turns_all)
    for level in range(2):
        for axis in range(3):
            parcel(level, axis, 1).start()
    for k in range(1, n_grp):
        gram_third(k).start()
    for axis in range(3):
        pack_into(recvs[axis], face_index(axis), axis, me, range(SIDE))

    def link(p, state):
        seen, order, last, before, users_of = state
        owner = wanted_tiles[p] // held
        hit = lane == owner
        turn = jnp.sum(jnp.where(hit, seen, 0), axis=1, keepdims=True)
        order = jnp.where(lane == p, owner * 2 + jnp.minimum(turn, 1), order)
        seen = jnp.where(hit, 1, seen)
        mine = lane == user_tiles[p]
        earlier = jnp.sum(jnp.where(mine, last, 0), axis=1, keepdims=True)
        before = jnp.where(lane == p, earlier, before)
        last = jnp.where(mine, p + 1, last)
        users_of = jnp.where(lane == p, user_tiles[p], users_of)
        return seen, order, last, before, users_of

    _, order, last, before, users_of = lax.fori_loop(0, pairs, link, (zero,) * 5)
    owner = order // 2
    owner_b, owner_g = owner // n_grp, owner % n_grp
    at, of = (owner_g // SIDE, owner_g % SIDE, owner_b // 2), owner_b % 2
    table[...] = jnp.zeros((8, 128), jnp.int32)
    table[1:2] = before
    table[2:3] = last
    table[3:4] = tile_place(users_of)
    for axis in range(3):
        face = (at[(axis + 1) % 3] * SIDE + at[(axis + 2) % 3]) * 2 + of
        ahead = (at[axis] + SIDE - place[axis]) % SIDE
        ahead = jnp.where(ahead >= 2, 5 - ahead, ahead)
        table[4 + axis:5 + axis] = face * SLOTS + ahead * 2 + order % 2
    table_copy = pltpu.make_async_copy(table, table_s, local_sems.at[2])
    table_copy.start()
    count_copy.wait()

    def weigh(p, carry):
        weight = counted[p].astype(jnp.float32) * ALPHA
        weights[p] = weight.astype(jnp.bfloat16)
        pulls[p] = jnp.where(weight > 0, 1.0 + weight, 0.0).astype(jnp.bfloat16)
        return carry

    lax.fori_loop(0, pairs, weigh, 0)
    for h in range(2):
        chain[h, 0] = jnp.zeros((half, rank), jnp.float32)
    table_copy.wait()

    gather_end(0)
    gather_end(1)
    for k in range(1, n_grp):
        gram_third(k).wait()

    def wait_parcel(step, carry):
        for level in range(2):
            for axis in range(3):
                parcel(level, axis, step).wait()
        return carry

    lax.fori_loop(1, FACE, wait_parcel, 0)

    def take(i, carry):
        for j in range(4):
            p = i * 4 + j
            for axis, (start, rows) in enumerate(SHARE):
                tiles[p, start:start + rows] = recvs[axis][table_s[4 + axis, p]]
        return carry

    lax.fori_loop(0, pairs // 4, take, 0)

    group = 8

    def score_all(h):
        part = slice(h * half, (h + 1) * half)

        def score(i, carry):
            for j in range(group):
                p = i * group + j
                scores = lax.dot_general(
                    lows[h][table_s[3, p]], tiles[p], (((1,), (1,)), ((), ())),
                    preferred_element_type=jnp.float32,
                )
                scaled[p, :half] = (weights[p, part].astype(jnp.float32) * scores).astype(jnp.bfloat16)
            return carry

        lax.fori_loop(0, pairs // group, score, 0)

    def spread_all(h):
        def spread(i, carry):
            backs = [
                jnp.dot(scaled[p, :half], tiles[p], preferred_element_type=jnp.float32)
                for p in (i * group + j for j in range(group))
            ]
            for j in range(group):
                p = i * group + j
                chain[h, p + 1] = chain[h, table_s[1, p]] + backs[j]
            return carry

        lax.fori_loop(0, pairs // group, spread, 0)

    def first_products():
        def score(i, carry):
            for j in range(group):
                p = i * group + j
                at = table_s[3, p]
                scores = lax.dot_general(
                    jnp.concatenate([lows[0][at], lows[1][at]], axis=0), tiles[p],
                    (((1,), (1,)), ((), ())), preferred_element_type=jnp.float32,
                )
                scaled[p] = (weights[p].astype(jnp.float32) * scores).astype(jnp.bfloat16)
            return carry

        lax.fori_loop(0, pairs // group, score, 0)

        def spread(i, carry):
            backs = []
            for j in range(group // 2):
                p = i * (group // 2) + j
                backs.append(
                    jnp.dot(pulls[p], tiles[p], preferred_element_type=jnp.float32)
                    - jnp.dot(scaled[p], tiles[p], preferred_element_type=jnp.float32)
                )
            for j in range(group // 2):
                p = i * (group // 2) + j
                for h in range(2):
                    part = backs[j][h * half:(h + 1) * half]
                    chain[h, p + 1] = chain[h, table_s[1, p]] + part
            return carry

        lax.fori_loop(0, pairs // (group // 2), spread, 0)

    near, far = (y, x), (x, y)

    def partial(h, t, away, end):
        u = 2 * (end * SIDE + away) if t == 0 else 2 * (away * SIDE + end) + 1
        return chain[h, table_s[2, u]]

    def sum_first(h, t, k, m):
        to = mesh_id(moved(place, 1 - t, k), core)
        return [
            remote(
                src.at[h, t, k, m], dst.at[h, t, k, m], first_sems.at[0, i, h, t, k, m],
                first_sems.at[1, i, h, t, k, m], to,
            )
            for i, (src, dst) in enumerate(((part_u, first_u), (part_q, first_q)))
        ]

    def sum_second(h, t, m):
        to = mesh_id(moved(place, t, m), core)
        return [
            remote(
                src.at[h, t, m], dst.at[h, t, m], second_sems.at[0, i, h, t, m],
                second_sems.at[1, i, h, t, m], to,
            )
            for i, (src, dst) in enumerate(((sum_u, second_u), (sum_q, second_q)))
        ]

    turns = tuple(range(1, SIDE)) + (0,)

    def reduce_begin(h):
        for m in turns:
            for k in range(1, SIDE):
                for t in range(2):
                    whole, unit = quantize(
                        partial(h, t, (near[t] + k) % SIDE, (far[t] + m) % SIDE)
                    )
                    part_q[h, t, k, m] = whole
                    part_u[h, t, k, m] = unit
                    for copy in sum_first(h, t, k, m):
                        copy.start()

    def reduce_onward(h):
        for m in turns:
            for t in range(2):
                total = partial(h, t, near[t], (far[t] + m) % SIDE)
                for k in range(1, SIDE):
                    for copy in sum_first(h, t, k, m):
                        copy.wait()
                    total = total + restore(first_q[h, t, k, m], first_u[h, t, k, m])
                if m == 0:
                    sums[h, t] = total
                else:
                    whole, unit = quantize(total)
                    sum_q[h, t, m] = whole
                    sum_u[h, t, m] = unit
                    for copy in sum_second(h, t, m):
                        copy.start()

    def reduce_end(h):
        totals = []
        for t in range(2):
            total = sums[h, t]
            for m in range(1, SIDE):
                for copy in sum_second(h, t, m):
                    copy.wait()
                total = total + restore(second_q[h, t, m], second_u[h, t, m])
            totals.append(total)
        return jnp.concatenate(totals, axis=0)

    def gram_term(vectors):
        return (
            jnp.dot(vectors, gram_c[...].reshape(rank, rank), precision=lax.Precision.HIGHEST,
                    preferred_element_type=jnp.float32)
            + REG * vectors
        )

    def row_sum(left, right):
        return jnp.sum(left * right, axis=1, keepdims=True)

    def products():
        score_all(0)
        gather_onward(1)
        spread_all(0)
        reduce_begin(0)
        gather_end(1)
        score_all(1)
        reduce_onward(0)
        spread_all(1)
        reduce_begin(1)

    def launch(h, vectors):
        lower(h, vectors)
        gather_begin(h)
        local[h] = gram_term(vectors)

    norms = []
    out[...] = prior[...]
    first_products()
    for h in range(2):
        reduce_begin(h)
    for h in range(2):
        local[h] = gram_term(half_rows(prior, h))
    reduce_onward(0)
    for h in range(2):
        if h == 1:
            reduce_onward(1)
            gather_onward(0)
        start = reduce_end(h) - local[h]
        residual[h] = start
        direction[h] = start
        norms.append(row_sum(start, start))
        launch(h, start)

    def iterate(step, norms):
        more = step < ITERS - 1
        gather_end(0)
        products()
        fresh = []
        for h in range(2):
            if h == 1:
                reduce_onward(1)
                pl.when(more)(functools.partial(gather_onward, 0))
            image = local[h] + reduce_end(h)
            d = direction[h]
            alpha = norms[h] / (row_sum(d, image) + EPS)
            for t in range(2):
                rows = slice(t * tile + h * half, t * tile + (h + 1) * half)
                block = slice(t * half, (t + 1) * half)
                out[rows] = out[rows] + alpha[block] * d[block]
            r = residual[h] - alpha * image
            residual[h] = r
            fresh.append(row_sum(r, r))
            after = r + fresh[h] / (norms[h] + EPS) * d
            direction[h] = after
            pl.when(more)(functools.partial(launch, h, after))

        return tuple(fresh)

    lax.fori_loop(0, ITERS, iterate, tuple(norms))


def body(user_prior, item_factors, user_tiles, item_tiles, counts):
    n_blk = lax.axis_size("blk")
    n_grp = lax.axis_size("grp")
    n_all = n_blk * n_grp
    pairs, tile, _ = counts.shape
    rank = item_factors.shape[1]
    users = 2 * n_grp
    own = user_prior.shape[0]
    held = item_factors.shape[0] // tile
    half = tile // 2
    grows = rank // n_grp
    vmem = pl.BlockSpec(memory_space=pltpu.VMEM)
    smem = pl.BlockSpec(memory_space=pltpu.SMEM)
    dma = pltpu.SemaphoreType.DMA
    low_type, whole_type, full = jnp.bfloat16, jnp.int16, jnp.float32
    return pl.pallas_call(
        functools.partial(kernel, n_blk, n_grp),
        out_shape=jax.ShapeDtypeStruct((own, rank), full),
        in_specs=[smem, smem, vmem, vmem, pl.BlockSpec(memory_space=pl.ANY)],
        out_specs=vmem,
        scratch_shapes=[
            pltpu.VMEM((1, 128), jnp.int32),
            pltpu.VMEM((n_all, 1, 128), jnp.int32),
            pltpu.SMEM((n_all, 1, 128), jnp.int32),
            pltpu.VMEM((8, 128), jnp.int32),
            pltpu.SMEM((8, 128), jnp.int32),
            *(pltpu.VMEM((CLOSE, held, rows, rank), low_type) for _, rows in SHARE),
            *(pltpu.VMEM((held, rows, rank), low_type) for _, rows in SHARE),
            *(pltpu.VMEM((FACE * SLOTS, rows, rank), low_type) for _, rows in SHARE),
            *(pltpu.VMEM((FACE * SLOTS, rows, rank), low_type) for _, rows in SHARE),
            pltpu.VMEM((pairs, tile, rank), low_type),
            pltpu.VMEM((pairs, tile, tile), jnp.int32),
            pltpu.VMEM((pairs, tile, tile), low_type),
            pltpu.VMEM((pairs, tile, tile), low_type),
            pltpu.VMEM((pairs, tile, tile), low_type),
            pltpu.VMEM((users, half, rank), low_type),
            pltpu.VMEM((users, half, rank), low_type),
            pltpu.VMEM((2, pairs + 1, half, rank), full),
            pltpu.VMEM((n_grp, grows, rank), full),
            pltpu.VMEM((n_grp, grows, rank), full),
            pltpu.VMEM((n_blk, grows, rank), full),
            pltpu.VMEM((n_grp, grows, rank), full),
            pltpu.VMEM((2, grows, rank), full),
            pltpu.VMEM((2, 2, SIDE, SIDE, half, rank), whole_type),
            pltpu.VMEM((2, 2, SIDE, SIDE, 1, rank), full),
            pltpu.VMEM((2, 2, SIDE, SIDE, half, rank), whole_type),
            pltpu.VMEM((2, 2, SIDE, SIDE, 1, rank), full),
            pltpu.VMEM((2, 2, SIDE, half, rank), whole_type),
            pltpu.VMEM((2, 2, SIDE, 1, rank), full),
            pltpu.VMEM((2, 2, SIDE, half, rank), whole_type),
            pltpu.VMEM((2, 2, SIDE, 1, rank), full),
            pltpu.VMEM((2, 2, half, rank), full),
            pltpu.VMEM((2, tile, rank), full),
            pltpu.VMEM((2, tile, rank), full),
            pltpu.VMEM((2, tile, rank), full),
            dma((2, PEERS)),
            dma((2, 3, 4)),
            dma((2, 2, 3, FACE)),
            dma((2, 2, 2, SIDE)),
            dma((2, 2, 2, SIDE, SIDE)),
            dma((2, 2, 2, 2, SIDE, SIDE)),
            dma((2, 2, 2, 2, SIDE)),
            dma((3, 2, n_grp)),
            dma((3,)),
        ],
        compiler_params=pltpu.CompilerParams(
            collective_id=0, has_side_effects=True, vmem_limit_bytes=60 << 20
        ),
        name="als",
    )(item_tiles, user_tiles, item_factors.reshape(held, tile, rank), user_prior, counts)


def solution(mesh):
    in_specs = (
        P(("blk", "grp"), None),
        P(("blk", "grp"), None),
        P(("blk", "grp")),
        P(("blk", "grp")),
        P(("blk", "grp"), None, None),
    )
    out_specs = P(("blk", "grp"), None)
    return jax.shard_map(body, mesh=mesh, in_specs=in_specs, out_specs=out_specs, check_vma=False)
```
